512 devices in a mesh: rep: 32 (over z, x), tp: 16 (over y, core).
Axes of the slice: x: 4, y: 8, z: 8, core: 2. Of those that a mesh axis runs over, the one named last changes fastest.
Arguments:
- tokens: bfloat16 [16384, 8192], P('rep', 'tp'), may hold values from -6 to 6
- frozen_weight: bfloat16 [8192, 2048], P('tp'), may hold values from -0.0625 to 0.0625
- cotangent: bfloat16 [16384, 2048], P('rep', 'tp'), may hold values from -6 to 6
- adapter_input_maps: bfloat16 [32, 16, 8192], P('rep', None, 'tp'), may hold values from -0.0625 to 0.0625
- adapter_output_maps: bfloat16 [32, 16, 2048], P('rep', None, 'tp'), may hold values from -0.375 to 0.375
- tenant: int32 [128], P('rep'), may hold values from 0 to 31
- adapter_storage_slot: int32 [32], replicated, may hold values from 0 to 31, each once
Outputs:
- projected: float32 [16384, 2048], P('rep', 'tp')
- token_gradient: float32 [16384, 8192], P('rep', 'tp')
- adapter_input_gradient: float32 [32, 16, 8192], P('rep', None, 'tp')
- adapter_output_gradient: float32 [32, 16, 2048], P('rep', None, 'tp')
The draws below stay inside these ranges and needn't reach their ends.
Inputs may be any that keep to these rules, and one draw needn't show every extreme that they name: `adapter_storage_slot`: each slot holds exactly one adapter.
All inputs are finite; a program needn't handle non-finite values.
Results may differ from the reference program's by a relative error of at most 0.00035.
Values may be sent and summed in bfloat16 or wider, within the bound.
A program may use at most 64 MiB of HBM per device.

```python
import math
import jax
import jax.numpy as jnp
import numpy as np
from jax import lax

MODEL_WIDTH = 8192
ADAPTER_RANK = 16
BLOCK = 128
KEY_VALUE_WIDTH = 2048
ADAPTER_COUNT = 32
TOKENS = 16384
NBLK = 128


def place_ends(entries, stream_key, least, largest):
    place = [jax.random.randint(jax.random.fold_in(stream_key, axis), (), 0, length) for axis, length in enumerate(entries.shape)]
    main_axis = entries.shape.index(max(entries.shape))
    beside = place[:main_axis] + [(place[main_axis] + 1) % entries.shape[main_axis]] + place[main_axis + 1:]
    return entries.at[tuple(place)].set(least).at[tuple(beside)].set(largest)


def block_scale(stream_key, extent, cuts, least, top_value):
    level = 1.0
    for axis_at, shards_of in cuts:
        steps = jax.random.uniform(jax.random.fold_in(jax.random.fold_in(stream_key, 6), axis_at), (shards_of,), jnp.float32, least / len(cuts), top_value / len(cuts))
        level = level * jnp.repeat(jnp.exp(steps), extent[axis_at] // shards_of).reshape((-1,) + (1,) * (len(extent) - 1 - axis_at))
    return level


def cumulative_ranks(number_of, lean):
    weights = [(1 << 20) // math.isqrt(standing ** lean) + 1 for standing in range(1, number_of + 1)]
    width = 1 + sum(weights) // (1 << 30)
    return np.cumsum(np.array([max(1, weight // width) for weight in weights]))


def ranked_ids(rng, extent, count, lean):
    listing = cumulative_ranks(count, lean)
    ticket = jax.random.randint(jax.random.fold_in(rng, 1), extent, 0, int(listing[count - 1]))
    rank = jnp.searchsorted(jnp.asarray(listing, jnp.int32), ticket, side="right")
    return jax.random.permutation(jax.random.fold_in(rng, 2), count)[rank].astype(jnp.int32)


def centred(rng, shape, spread, most, pieces=(), kind=jnp.bfloat16):
    entries = spread * jax.random.normal(rng, shape, jnp.float32)
    if pieces:
        entries = entries * block_scale(rng, shape, pieces, -0.22, 0.18)
    return jnp.clip(entries, -most, most).astype(kind)


def setup_inputs(seed: int = 0) -> dict:
    keys = jax.random.split(jax.random.key(seed), 8)
    return {
        "tokens": centred(keys[0], (TOKENS, MODEL_WIDTH), 1.0, 6.0, ((0, 32), (1, 16))),
        "frozen_weight": centred(keys[1], (MODEL_WIDTH, KEY_VALUE_WIDTH), MODEL_WIDTH ** -0.5, 0.0625, ((0, 16),)),
        "cotangent": centred(keys[2], (TOKENS, KEY_VALUE_WIDTH), 1.0, 6.0, ((0, 32), (1, 16))),
        "adapter_input_maps": centred(keys[3], (ADAPTER_COUNT, ADAPTER_RANK, MODEL_WIDTH), MODEL_WIDTH ** -0.5, 0.0625, ((0, 32), (2, 16))),
        "adapter_output_maps": centred(keys[4], (ADAPTER_COUNT, ADAPTER_RANK, KEY_VALUE_WIDTH), (16 * ADAPTER_RANK) ** -0.5, 0.375, ((0, 32), (2, 16))),
        "tenant": place_ends(ranked_ids(keys[5], (NBLK,), ADAPTER_COUNT, 2), jax.random.fold_in(keys[5], 3), 0, ADAPTER_COUNT - 1).astype(jnp.int32),
        "adapter_storage_slot": jax.random.permutation(keys[6], ADAPTER_COUNT).astype(jnp.int32),
    }


HIGH_ACCURACY = lax.Precision.HIGHEST


def reference(tokens, frozen_weight, cotangent, adapter_input_maps, adapter_output_maps, tenant, adapter_storage_slot):
    adapter_list = adapter_input_maps.shape[0]
    blocks = tenant.shape[0]
    block_storage_slot = adapter_storage_slot[tenant]
    input_map_rows = adapter_input_maps[block_storage_slot].astype(jnp.float32)
    output_map_rows = adapter_output_maps[block_storage_slot].astype(jnp.float32)
    token_rows = tokens.reshape(blocks, BLOCK, MODEL_WIDTH).astype(jnp.float32)
    rank_in = jnp.einsum('bnd,brd->bnr', token_rows, input_map_rows, precision=HIGH_ACCURACY)
    base = jnp.dot(tokens, frozen_weight, preferred_element_type=jnp.float32)
    low_rank = 2.0 * jnp.einsum('bnr,brc->bnc', rank_in, output_map_rows, precision=HIGH_ACCURACY)
    projected = base + low_rank.reshape(-1, KEY_VALUE_WIDTH)
    grad_rows = cotangent.reshape(blocks, BLOCK, KEY_VALUE_WIDTH).astype(jnp.float32)
    rank_back = jnp.einsum('bnc,brc->bnr', grad_rows, output_map_rows, precision=HIGH_ACCURACY)
    through = jnp.dot(cotangent, frozen_weight.T, preferred_element_type=jnp.float32)
    side = 2.0 * jnp.einsum('bnr,brd->bnd', rank_back, input_map_rows, precision=HIGH_ACCURACY)
    token_gradient = through + side.reshape(-1, MODEL_WIDTH)
    input_map_gradient = 2.0 * jnp.einsum('bnr,bnd->brd', rank_back, token_rows, precision=HIGH_ACCURACY)
    output_map_gradient = 2.0 * jnp.einsum('bnr,bnc->brc', rank_in, grad_rows, precision=HIGH_ACCURACY)
    tenant_selector = (block_storage_slot[:, None] == jnp.arange(adapter_list, dtype=jnp.int32)[None, :]).astype(jnp.float32)
    counts = BLOCK * jnp.sum(tenant_selector, axis=0)
    adapter_scale = 1.0 / jnp.maximum(counts, 1.0)
    adapter_input_gradient = jnp.einsum('ol,oht->lht', tenant_selector, input_map_gradient, precision=HIGH_ACCURACY) * adapter_scale[:, None, None]
    adapter_output_gradient = jnp.einsum('pa,pne->ane', tenant_selector, output_map_gradient, precision=HIGH_ACCURACY) * adapter_scale[:, None, None]
    return (projected, token_gradient, adapter_input_gradient, adapter_output_gradient)
```

```python
import functools

import jax
import jax.numpy as jnp
from jax import lax
from jax.experimental import pallas as pl
from jax.experimental.pallas import tpu as pltpu
from jax.sharding import PartitionSpec as P

MESH = pl.DeviceIdType.MESH
F32, BF16 = jnp.float32, jnp.bfloat16
NX, NY, NZ, NC = 4, 8, 8, 2
NT = NY * NC
BLOCK = 128
NT_DIMS = (((1,), (1,)), ((), ()))
TN_DIMS = (((0,), (0,)), ((), ()))


def dot(a, b):
    return jnp.dot(a, b, preferred_element_type=F32)


def dot_nt(a, b):
    return lax.dot_general(a, b, NT_DIMS, preferred_element_type=F32)


def dot_tn(a, b):
    return lax.dot_general(a, b, TN_DIMS, preferred_element_type=F32)


def two_parts(v):
    high = v.astype(BF16)
    low = (v - high.astype(F32)).astype(BF16)
    return jnp.concatenate([high, low], axis=0)


def kernel(
    tenant, storage, tok, w, cot, ain, aout,
    proj, tgrad, gin, gout,
    maps, sel, cnt, cotf, tokp, wp, base, rs_right, rs_left,
    part, part_in, full, gx, gz_out, gz_in,
    ssem, rsem, lsem,
):
    r, t = lax.axis_index("rep"), lax.axis_index("tp")
    z, x = lax.div(r, NX), lax.rem(r, NX)
    y, c = lax.div(t, NC), lax.rem(t, NC)
    rows = tok.shape[0]
    half = rows // 2
    nb = rows // BLOCK
    feat = tok.shape[1]
    rank = ain.shape[1]
    grouped = feat + cot.shape[1]
    other = 1 - c

    def at_y(d):
        return (r, lax.rem(y + d + NY, NY) * NC + c)

    def at_x(d):
        return (z * NX + lax.rem(x + d + NX, NX), t)

    def at_z(d):
        return (lax.rem(z + d + NZ, NZ) * NX + x, t)

    mate = (r, y * NC + other)
    counter = [0]
    sent = []

    def copy_to(src, dst, device):
        i = counter[0]
        counter[0] += 1
        made = pltpu.make_async_remote_copy(
            src_ref=src, dst_ref=dst, send_sem=ssem.at[i], recv_sem=rsem.at[i],
            device_id=device, device_id_type=MESH,
        )
        made.start()
        sent.append(made)
        return made

    local = [
        pltpu.make_async_copy(ain.at[0], maps.at[r, :, pl.ds(0, feat)], lsem.at[0]),
        pltpu.make_async_copy(aout.at[0], maps.at[r, :, pl.ds(feat, grouped - feat)], lsem.at[1]),
        pltpu.make_async_copy(cot, cotf.at[y, :, pl.ds(pl.multiple_of(c * 128, 128), 128)], lsem.at[2]),
    ]
    for made in local:
        made.start()
    lane = lax.broadcasted_iota(jnp.int32, (1, 128), 1)
    slots = [storage[tenant[b]] for b in range(nb)]
    for b in range(nb):
        sel[0, b:b + 1, :] = jnp.where(lane == slots[b], 1.0, 0.0).astype(F32)

    barrier = pltpu.get_barrier_semaphore()
    greeted = [mate, at_y(1), at_y(-1), at_x(1), at_x(2), at_x(3), at_z(1), at_z(-1)]
    for device in greeted:
        pl.semaphore_signal(barrier, inc=1, device_id=device, device_id_type=MESH)
    pl.semaphore_wait(barrier, len(greeted))
    for made in local:
        made.wait()

    maps_x = [copy_to(maps.at[r], maps.at[r], at_x(k)) for k in (1, 2, 3)]
    sel_x = [copy_to(sel.at[0], sel.at[k], at_x(k)) for k in (1, 2, 3)]

    def cot_at(yy, cc, lo, size):
        return cotf.at[yy, pl.ds(lo, size), pl.ds(pl.multiple_of(cc * 128, 128), 128)]

    ag_right, ag_left, ag_mate = {}, {}, []
    ag_right[1] = copy_to(cot, cot_at(y, c, 0, rows), at_y(1))
    ag_left[1] = copy_to(cot, cot_at(y, c, 0, rows), at_y(-1))
    tok_mate = copy_to(tok, tokp, mate)
    order = (4, 3, 5, 2, 6, 1, 7, 0)
    w_mate = {}

    def w_cols(d, cc):
        yy = lax.rem(y + d, NY)
        return pl.ds(pl.multiple_of(yy * (NC * 128) + cc * 128, 128), 128)

    for d in order:
        w_mate[d] = copy_to(w.at[:, w_cols(d, other)], wp.at[d], mate)
    ag_mate.append(copy_to(cot, cot_at(y, c, 0, rows), mate))

    for d in order:
        base[d] = dot(tok[...], w[:, w_cols(d, c)])

    for made in maps_x:
        made.wait_recv()
    mz_right, mz_left = {}, {}

    def maps_at(zz, lo, size):
        return maps.at[pl.ds(lax.rem(zz + NZ, NZ) * NX + lo, size)]

    mz_right[1] = copy_to(maps_at(z, 0, NX), maps_at(z, 0, NX), at_z(1))
    mz_left[1] = copy_to(maps_at(z, 0, NX), maps_at(z, 0, NX), at_z(-1))

    def ag_step(s):
        ag_right[s].wait_recv()
        ag_left[s].wait_recv()
        lo_y, hi_y = lax.rem(y - s + NY, NY), lax.rem(y + s, NY)
        size = rows if s < 3 else half
        piece = cot_at(lo_y, c, 0, size)
        ag_right[s + 1] = copy_to(piece, piece, at_y(1))
        piece = cot_at(hi_y, c, rows - size, size)
        ag_left[s + 1] = copy_to(piece, piece, at_y(-1))
        for yy in (lo_y, hi_y):
            piece = cot_at(yy, c, 0, rows)
            ag_mate.append(copy_to(piece, piece, mate))

    def mz_step(s):
        mz_right[s].wait_recv()
        mz_left[s].wait_recv()
        size = NX if s < 3 else NX // 2
        piece = maps_at(z - s, 0, size)
        mz_right[s + 1] = copy_to(piece, piece, at_z(1))
        piece = maps_at(z + s, NX - size, size)
        mz_left[s + 1] = copy_to(piece, piece, at_z(-1))

    rs = {}

    def rs_rows(h):
        return pl.ds(0 if h == "A" else half, half)

    def rs_send(way, h, d):
        slot = len([k for k in rs if k[0] == way])
        target = rs_right if way > 0 else rs_left
        made = copy_to(base.at[(way * d) % NY, rs_rows(h)], target.at[slot], at_y(way))
        rs[way, h, d] = (made, slot)

    def rs_take(way, h, d):
        made, slot = rs[way, h, d]
        made.wait_recv()
        source = rs_right if way > 0 else rs_left
        base[(way * (d - 1)) % NY, rs_rows(h)] += source[slot]

    def rs_hop(d, first):
        right, left = ("A", "B") if first else ("B", "A")
        rs_take(1, right, d + 1)
        rs_send(1, right, d)
        rs_take(-1, left, d + 1)
        rs_send(-1, left, d)

    def add_mate(d):
        w_mate[d].wait_recv()
        base[d] += dot(tokp[...], wp[d])

    ag_step(1)
    tok_mate.wait_recv()
    add_mate(4)
    rs_send(1, "A", 4)
    rs_send(-1, "B", 4)
    add_mate(3)
    rs_send(1, "B", 3)
    add_mate(5)
    rs_send(-1, "A", 3)
    mz_step(1)
    ag_step(2)
    add_mate(2)
    add_mate(6)
    mz_step(2)
    rs_hop(3, True)
    ag_step(3)
    for d in (1, 7, 0):
        add_mate(d)
    rs_hop(2, False)
    mz_step(3)

    ag_mate[0].wait_recv()
    tgrad[...] = dot_nt(cotf[y], w[:, pl.ds(pl.multiple_of(y * 256, 256), 256)])

    def through(yy):
        tgrad[...] += dot_nt(cotf[yy], w[:, pl.ds(pl.multiple_of(yy * 256, 256), 256)])

    ag_right[4].wait_recv()
    ag_left[4].wait_recv()
    far = cot_at(lax.rem(y + 4, NY), c, 0, rows)
    ag_mate.append(copy_to(far, far, mate))

    mz_right[4].wait_recv()
    mz_left[4].wait_recv()

    chosen = [maps[slots[b]] for b in range(nb)]
    for b in range(nb):
        here = pl.ds(b * BLOCK, BLOCK)
        pin = dot_nt(chosen[b][:, :feat], tok[here, :])
        pback = dot_nt(chosen[b][:, feat:], cot[here, :])
        part[b] = pin[:8]
        part[nb + b] = pin[8:]
        part[2 * nb + b] = pback[:8]
        part[3 * nb + b] = pback[8:]
    sums = []
    for k in range(1, NT):
        tt = lax.rem(t + k, NT)
        sums.append(copy_to(part.at[tt], part_in.at[k], (r, tt)))

    for made in sel_x:
        made.wait_recv()
    cnt[0] = jnp.sum(jnp.sum(sel[...], axis=0), axis=0, keepdims=True)
    counted = [copy_to(cnt.at[0], cnt.at[k], at_z(k)) for k in range(1, NZ)]

    rs_hop(2, True)

    total = part[t]
    for made in sums:
        made.wait_recv()
    for k in range(1, NT):
        total = total + part_in[k]
    full[t] = total
    spread = [copy_to(full.at[t], full.at[t], (r, lax.rem(t + k, NT))) for k in range(1, NT)]

    rs_hop(1, False)
    for i, s in ((1, 1), (2, -1)):
        ag_mate[i].wait_recv()
        through(lax.rem(y - s + NY, NY))

    for made in spread:
        made.wait_recv()
    rin = [two_parts(jnp.concatenate([full[b], full[nb + b]], axis=0)) for b in range(nb)]
    rback = [two_parts(jnp.concatenate([full[2 * nb + b], full[3 * nb + b]], axis=0)) for b in range(nb)]
    for b in range(nb):
        here = pl.ds(b * BLOCK, BLOCK)
        da = dot(rback[b], tok[here, :])
        db = dot(rin[b], cot[here, :])
        gx[0, b, :, :feat] = da[:rank] + da[rank:]
        gx[0, b, :, feat:] = db[:rank] + db[rank:]
    grads_x = [copy_to(gx.at[0], gx.at[k], at_x(k)) for k in (1, 2, 3)]

    rs_hop(1, True)
    for b in range(nb):
        here = pl.ds(b * BLOCK, BLOCK)
        amap = jnp.concatenate([chosen[b][:, :feat]] * 2, axis=0)
        bmap = jnp.concatenate([chosen[b][:, feat:]] * 2, axis=0)
        tgrad[here, :] += 2.0 * dot_tn(rback[b], amap)
        base[0, here, :] += 2.0 * dot_tn(rin[b], bmap)
    for i, s in ((3, 2), (4, -2)):
        ag_mate[i].wait_recv()
        through(lax.rem(y - s + NY, NY))

    for made in grads_x:
        made.wait_recv()
    grads_z = []
    for d in (4, 3, 5, 2, 6, 1, 7, 0):
        owner = lax.rem(z + d, NZ) * NX + x
        acc = jnp.zeros((rank, grouped), F32)
        for k in range(NX):
            weight = jnp.sum(jnp.where(lane == owner, sel[k], 0.0), axis=1, keepdims=True)
            for b in range(nb):
                acc = acc + weight[b:b + 1, :] * gx[k, b]
        gz_out[d] = acc
        if d:
            grads_z.append(copy_to(gz_out.at[d], gz_in.at[d], at_z(d)))

    for i, s in ((5, 3), (6, -3), (7, 4)):
        ag_mate[i].wait_recv()
        through(lax.rem(y - s + NY, NY))

    for way, first, second in ((1, "B", "A"), (-1, "A", "B")):
        rs_take(way, first, 1)
    for way, second in ((1, "A"), (-1, "B")):
        rs_take(way, second, 1)
    proj[...] = base[0]

    for made in counted:
        made.wait_recv()
    blocks_of = jnp.sum(cnt[...], axis=0)
    mine = jnp.sum(jnp.where(lane == r, blocks_of, 0.0), axis=1, keepdims=True)
    scale = 2.0 / jnp.maximum(mine * float(BLOCK), 1.0)
    for made in grads_z:
        made.wait_recv()
    acc = gz_out[0]
    for d in range(1, NZ):
        acc = acc + gz_in[d]
    acc = acc * scale
    gin[0] = acc[:, :feat]
    gout[0] = acc[:, feat:]
    for made in sent:
        made.wait_send()


COPIES = 128


def shards(tok, w, cot, ain, aout, tenant, storage):
    rows, feat = tok.shape
    cols = cot.shape[1]
    rank = ain.shape[1]
    nb = tenant.shape[0]
    grouped = feat + cols
    vmem = pl.BlockSpec(memory_space=pltpu.VMEM)
    smem = pl.BlockSpec(memory_space=pltpu.SMEM)
    return pl.pallas_call(
        kernel,
        out_shape=(
            jax.ShapeDtypeStruct((rows, cols), F32),
            jax.ShapeDtypeStruct((rows, feat), F32),
            jax.ShapeDtypeStruct(ain.shape, F32),
            jax.ShapeDtypeStruct(aout.shape, F32),
        ),
        in_specs=[smem, smem] + [vmem] * 5,
        out_specs=[vmem] * 4,
        scratch_shapes=[
            pltpu.VMEM((NX * NZ, rank, grouped), BF16),
            pltpu.VMEM((NX, nb, 128), F32),
            pltpu.VMEM((NZ, 1, 128), F32),
            pltpu.VMEM((NY, rows, NC * cols), BF16),
            pltpu.VMEM((rows, feat), BF16),
            pltpu.VMEM((NY, feat, cols), BF16),
            pltpu.VMEM((NY, rows, cols), F32),
            pltpu.VMEM((7, rows // 2, cols), F32),
            pltpu.VMEM((7, rows // 2, cols), F32),
            pltpu.VMEM((NT, 8, 128), F32),
            pltpu.VMEM((NT, 8, 128), F32),
            pltpu.VMEM((NT, 8, 128), F32),
            pltpu.VMEM((NX, nb, rank, grouped), F32),
            pltpu.VMEM((NZ, rank, grouped), F32),
            pltpu.VMEM((NZ, rank, grouped), F32),
            pltpu.SemaphoreType.DMA((COPIES,)),
            pltpu.SemaphoreType.DMA((COPIES,)),
            pltpu.SemaphoreType.DMA((3,)),
        ],
        compiler_params=pltpu.CompilerParams(
            collective_id=0, has_side_effects=True, vmem_limit_bytes=56 * 1024 * 1024
        ),
    )(tenant, storage, tok, w, cot, ain, aout)


def solution(mesh):
    placed = (
        P("rep", "tp"),
        P("tp", None),
        P("rep", "tp"),
        P("rep", None, "tp"),
        P("rep", None, "tp"),
        P("rep"),
        P(),
    )
    return jax.shard_map(
        shards,
        mesh=mesh,
        in_specs=placed,
        out_specs=(P("rep", "tp"), P("rep", "tp"), P("rep", None, "tp"), P("rep", None, "tp")),
        check_vma=False,
    )
```

```python
import functools

import jax
import jax.numpy as jnp
from jax import lax
from jax.experimental import pallas as pl
from jax.experimental.pallas import tpu as pltpu
from jax.sharding import PartitionSpec as P

MESH = pl.DeviceIdType.MESH
F32, BF16 = jnp.float32, jnp.bfloat16
NX, NY, NZ, NC = 4, 8, 8, 2
NT = NY * NC
BLOCK = 128
NT_DIMS = (((1,), (1,)), ((), ()))
TN_DIMS = (((0,), (0,)), ((), ()))


def dot(a, b):
    return jnp.dot(a, b, preferred_element_type=F32)


def dot_nt(a, b):
    return lax.dot_general(a, b, NT_DIMS, preferred_element_type=F32)


def dot_tn(a, b):
    return lax.dot_general(a, b, TN_DIMS, preferred_element_type=F32)


def two_parts(v):
    high = v.astype(BF16)
    low = (v - high.astype(F32)).astype(BF16)
    return jnp.concatenate([high, low], axis=0)


def encode(v):
    top = jnp.max(jnp.max(jnp.abs(v), axis=0, keepdims=True), axis=1, keepdims=True)
    e = jnp.floor(jnp.log2(jnp.maximum(top, 1e-30)))
    scale = jnp.exp2(6.0 - e).astype(BF16).astype(F32)
    inverse = jnp.exp2(e - 6.0).astype(BF16).astype(F32)
    u = v * scale
    p = u * u
    p = p * p
    p = p * p
    p = p * p
    return jnp.where(u < 0, -p, p).astype(BF16), inverse


def decode(code, inverse):
    y = code.astype(F32)
    p = lax.rsqrt(lax.rsqrt(lax.rsqrt(lax.rsqrt(jnp.abs(y)))))
    return jnp.where(y < 0, -p, p) * inverse


def encode_grads(v, feat):
    left, linv = encode(v[:, :feat])
    right, rinv = encode(v[:, feat:])
    rank = v.shape[0]
    tail = jnp.concatenate(
        [jnp.broadcast_to(linv, (rank, 64)), jnp.broadcast_to(rinv, (rank, 64))], axis=1
    )
    return jnp.concatenate([left, right, tail.astype(BF16)], axis=1)


def decode_grads(m, feat):
    grouped = m.shape[1] - 128
    linv = m[0:1, grouped:grouped + 1].astype(F32)
    rinv = m[0:1, grouped + 64:grouped + 65].astype(F32)
    return decode(m[:, :feat], linv), decode(m[:, feat:grouped], rinv)


def kernel(
    tenant, storage, tok_in, w_in, cot_in, ain, aout,
    proj, tgrad_out, gin, gout,
    tok, w, cot, tgrad, gtotal,
    maps, sel, cnt, cotf, tokp, wp, base, rs_out, rs_right, rs_left,
    part, part_in, full, gx, gown, gz_out, gz_in,
    ssem, rsem, lsem,
):
    r, t = lax.axis_index("rep"), lax.axis_index("tp")
    z, x = lax.div(r, NX), lax.rem(r, NX)
    y, c = lax.div(t, NC), lax.rem(t, NC)
    rows = tok.shape[0]
    half = rows // 2
    nb = rows // BLOCK
    feat = tok.shape[1]
    rank = ain.shape[1]
    grouped = feat + cot.shape[1]
    other = 1 - c

    def at_y(d):
        return (r, lax.rem(y + d + NY, NY) * NC + c)

    def at_x(d):
        return (z * NX + lax.rem(x + d + NX, NX), t)

    def at_z(d):
        return (lax.rem(z + d + NZ, NZ) * NX + x, t)

    mate = (r, y * NC + other)
    counter = [0]
    sent = []

    def copy_to(src, dst, device):
        i = counter[0]
        counter[0] += 1
        made = pltpu.make_async_remote_copy(
            src_ref=src, dst_ref=dst, send_sem=ssem.at[i], recv_sem=rsem.at[i],
            device_id=device, device_id_type=MESH,
        )
        made.start()
        sent.append(made)
        return made

    own_lanes = pl.ds(pl.multiple_of(c * 128, 128), 128)
    local = [
        pltpu.make_async_copy(ain.at[0], maps.at[r, :, pl.ds(0, feat)], lsem.at[0]),
        pltpu.make_async_copy(aout.at[0], maps.at[r, :, pl.ds(feat, grouped - feat)], lsem.at[1]),
        pltpu.make_async_copy(cot_in, cot, lsem.at[2]),
        pltpu.make_async_copy(cot_in, cotf.at[y, :, own_lanes], lsem.at[3]),
        pltpu.make_async_copy(tok_in, tok, lsem.at[4]),
        pltpu.make_async_copy(w_in, w, lsem.at[5]),
    ]
    for made in local:
        made.start()

    barrier = pltpu.get_barrier_semaphore()
    greeted = [at_z(k) for k in (4, 3, 5, 2, 6, 1, 7)] + [at_x(2), at_x(1), at_x(3), at_y(1), at_y(-1), mate]
    for device in greeted:
        pl.semaphore_signal(barrier, inc=1, device_id=device, device_id_type=MESH)
    lane = lax.broadcasted_iota(jnp.int32, (1, 128), 1)
    slots = [storage[tenant[b]] for b in range(nb)]
    for b in range(nb):
        sel[0, b:b + 1, :] = jnp.where(lane == slots[b], 1.0, 0.0).astype(F32)
    for made in local:
        made.wait()
    pl.semaphore_wait(barrier, len(greeted))

    maps_z = {k: copy_to(maps.at[r], maps.at[r], at_z(k)) for k in (4, 3, 5, 2, 6, 1, 7)}
    maps_x = [copy_to(maps.at[r], maps.at[r], at_x(k)) for k in (2, 1, 3)]

    def cot_at(yy, cc, lo, size):
        return cotf.at[yy, pl.ds(lo, size), pl.ds(pl.multiple_of(cc * 128, 128), 128)]

    ag_right, ag_left, ag_mate = {}, {}, []
    ag_right[1] = copy_to(cot, cot_at(y, c, 0, rows), at_y(1))
    ag_left[1] = copy_to(cot, cot_at(y, c, 0, rows), at_y(-1))
    tok_mate = copy_to(tok, tokp, mate)
    pairs = ((4, 3), (5, 2), (6, 1), (7, 0))
    w_mate = {}

    def w_cols(d, cc):
        yy = lax.rem(y + d, NY)
        return pl.ds(pl.multiple_of(yy * (NC * 128) + cc * 128, 128), 128)

    for d in (4, 3, 5, 2, 6, 1, 7, 0):
        w_mate[d] = copy_to(w.at[:, w_cols(d, other)], wp.at[d], mate)
    ag_mate.append(copy_to(cot, cot_at(y, c, 0, rows), mate))
    sel_x = [copy_to(sel.at[0], sel.at[k], at_x(k)) for k in (1, 2, 3)]

    def own_pair(pair):
        both = dot(tok[...], jnp.concatenate([w[:, w_cols(d, c)] for d in pair], axis=1))
        base[pair[0]] = both[:, :128]
        base[pair[1]] = both[:, 128:]

    def mate_pair(pair):
        for d in pair:
            w_mate[d].wait_recv()
        both = dot(tokp[...], jnp.concatenate([wp[d] for d in pair], axis=1))
        base[pair[0]] += both[:, :128]
        base[pair[1]] += both[:, 128:]

    def maps_on(*ks):
        for k in ks:
            maps_z[k].wait_recv()
            came = maps.at[lax.rem(z - k + NZ, NZ) * NX + x]
            for j in (2, 1, 3):
                maps_x.append(copy_to(came, came, at_x(j)))

    def ag_step(s):
        ag_right[s].wait_recv()
        ag_left[s].wait_recv()
        lo_y, hi_y = lax.rem(y - s + NY, NY), lax.rem(y + s, NY)
        size = rows if s < 3 else half
        piece = cot_at(lo_y, c, 0, size)
        ag_right[s + 1] = copy_to(piece, piece, at_y(1))
        piece = cot_at(hi_y, c, rows - size, size)
        ag_left[s + 1] = copy_to(piece, piece, at_y(-1))
        for yy in (lo_y, hi_y):
            piece = cot_at(yy, c, 0, rows)
            ag_mate.append(copy_to(piece, piece, mate))

    rs = {}

    def rs_rows(h):
        return pl.ds(0 if h == "A" else half, half)

    def rs_send(way, h, d):
        slot = len([k for k in rs if k[0] == way])
        target = rs_right if way > 0 else rs_left
        place = slot + (7 if way < 0 else 0)
        code, inverse = encode(base[(way * d) % NY, rs_rows(h), :])
        rs_out[place, :half, :] = code
        rs_out[place, half:, :] = jnp.broadcast_to(inverse, (16, 128)).astype(BF16)
        made = copy_to(rs_out.at[place], target.at[slot], at_y(way))
        rs[way, h, d] = (made, slot)

    def rs_take(way, h, d):
        made, slot = rs[way, h, d]
        made.wait_recv()
        source = rs_right if way > 0 else rs_left
        inverse = source[slot, half:half + 1, :].astype(F32)
        base[(way * (d - 1)) % NY, rs_rows(h), :] += decode(source[slot, :half, :], inverse)

    def rs_hop(d, first):
        right, left = ("A", "B") if first else ("B", "A")
        rs_take(1, right, d + 1)
        rs_send(1, right, d)
        rs_take(-1, left, d + 1)
        rs_send(-1, left, d)

    def through(yy):
        tgrad[...] += dot_nt(cotf[yy], w[:, pl.ds(pl.multiple_of(yy * 256, 256), 256)])

    def through_steps(*pieces):
        for i, s in pieces:
            ag_mate[i].wait_recv()
            through(lax.rem(y - s + NY, NY))

    own_pair(pairs[0])
    own_pair(pairs[1])
    maps_on(1, 7, 2, 6)
    own_pair(pairs[2])
    maps_on(3, 5, 4)
    ag_step(1)
    tok_mate.wait_recv()
    mate_pair(pairs[0])
    rs_send(1, "A", 4)
    rs_send(-1, "B", 4)
    rs_send(1, "B", 3)
    mate_pair(pairs[1])
    rs_send(-1, "A", 3)
    own_pair(pairs[3])
    ag_step(2)

    for made in maps_x:
        made.wait_recv()
    chosen = [maps[slots[b]] for b in range(nb)]
    for b in range(0, nb, 2):
        here = pl.ds(b * BLOCK, 2 * BLOCK)
        two = jnp.concatenate([chosen[b], chosen[b + 1]], axis=0)
        pin = dot_nt(two[:, :feat], tok[here, :])
        pback = dot_nt(two[:, feat:], cot[here, :])
        for i in range(2):
            mine = slice(i * BLOCK, (i + 1) * BLOCK)
            part[b + i] = pin[rank * i:rank * i + 8, mine]
            part[nb + b + i] = pin[rank * i + 8:rank * i + 16, mine]
            part[2 * nb + b + i] = pback[rank * i:rank * i + 8, mine]
            part[3 * nb + b + i] = pback[rank * i + 8:rank * i + 16, mine]

    ag_step(3)
    ag_right[4].wait_recv()
    ag_left[4].wait_recv()
    far = cot_at(lax.rem(y + 4, NY), c, 0, rows)
    ag_mate.append(copy_to(far, far, mate))

    sums = []
    for k in (8, 7, 9, 6, 10, 5, 11, 4, 12, 3, 13, 2, 14, 1, 15):
        tt = lax.rem(t + k, NT)
        sums.append(copy_to(part.at[tt], part_in.at[k], (r, tt)))

    for made in sel_x:
        made.wait_recv()
    cnt[0] = jnp.sum(jnp.sum(sel[...], axis=0), axis=0, keepdims=True)
    counted = [copy_to(cnt.at[0], cnt.at[k], at_z(k)) for k in range(1, NZ)]

    mate_pair(pairs[2])
    rs_hop(3, True)
    rs_hop(2, False)

    total = part[t]
    for made in sums:
        made.wait_recv()
    for k in range(1, NT):
        total = total + part_in[k]
    full[t] = total
    spread = []
    for k in (8, 7, 9, 6, 10, 5, 11, 4, 12, 3, 13, 2, 14, 1, 15):
        spread.append(copy_to(full.at[t], full.at[t], (r, lax.rem(t + k, NT))))

    mate_pair(pairs[3])
    rs_hop(2, True)
    ag_mate[0].wait_recv()
    tgrad[...] = dot_nt(cotf[y], w[:, pl.ds(pl.multiple_of(y * 256, 256), 256)])
    through_steps((1, 1), (2, -1))

    for made in spread:
        made.wait_recv()
    rin = [two_parts(jnp.concatenate([full[b], full[nb + b]], axis=0)) for b in range(nb)]
    rback = [two_parts(jnp.concatenate([full[2 * nb + b], full[3 * nb + b]], axis=0)) for b in range(nb)]
    for b in range(nb):
        here = pl.ds(b * BLOCK, BLOCK)
        da = dot(rback[b], tok[here, :])
        db = dot(rin[b], cot[here, :])
        own = jnp.concatenate([da[:rank] + da[rank:], db[:rank] + db[rank:]], axis=1)
        gown[b] = own
        gx[0, b] = encode_grads(own, feat)
    grads_x = [copy_to(gx.at[0], gx.at[k], at_x(k)) for k in (2, 1, 3)]

    rs_hop(1, False)
    for b in range(nb):
        here = pl.ds(b * BLOCK, BLOCK)
        amap = jnp.concatenate([chosen[b][:, :feat]] * 2, axis=0)
        bmap = jnp.concatenate([chosen[b][:, feat:]] * 2, axis=0)
        tgrad[here, :] += 2.0 * dot_tn(rback[b], amap)
        base[0, here, :] += 2.0 * dot_tn(rin[b], bmap)
    rs_hop(1, True)
    through_steps((3, 2), (4, -2))

    for made in grads_x:
        made.wait_recv()
    for k in range(1, NX):
        for b in range(nb):
            one, two = decode_grads(gx[k, b], feat)
            gown[k * nb + b, :, :feat] = one
            gown[k * nb + b, :, feat:] = two
    grads_z = {}
    for d in (4, 3, 5, 2, 6, 1, 7, 0):
        owner = lax.rem(z + d, NZ) * NX + x
        acc = jnp.zeros((rank, grouped), F32)
        for k in range(NX):
            weight = jnp.sum(jnp.where(lane == owner, sel[k], 0.0), axis=1, keepdims=True)
            for b in range(nb):
                acc = acc + weight[b:b + 1, :] * gown[k * nb + b]
        if d:
            gz_out[d] = encode_grads(acc, feat)
            grads_z[d] = copy_to(gz_out.at[d], gz_in.at[d], at_z(d))
        else:
            gtotal[...] = acc

    through_steps((5, 3), (6, -3), (7, 4))
    out_tg = pltpu.make_async_copy(tgrad, tgrad_out, lsem.at[0])
    out_tg.start()

    rs_take(1, "B", 1)
    rs_take(-1, "A", 1)
    rs_take(1, "A", 1)
    rs_take(-1, "B", 1)
    out_pj = pltpu.make_async_copy(base.at[0], proj, lsem.at[1])
    out_pj.start()

    for made in counted:
        made.wait_recv()
    blocks_of = jnp.sum(cnt[...], axis=0)
    mine = jnp.sum(jnp.where(lane == r, blocks_of, 0.0), axis=1, keepdims=True)
    scale = 2.0 / jnp.maximum(mine * float(BLOCK), 1.0)
    acc_in, acc_out = gtotal[:, :feat], gtotal[:, feat:]
    for d in (1, 7, 2, 6, 3, 5, 4):
        grads_z[d].wait_recv()
        one, two = decode_grads(gz_in[d], feat)
        acc_in, acc_out = acc_in + one, acc_out + two
    gtotal[:, :feat] = acc_in * scale
    gtotal[:, feat:] = acc_out * scale
    out_gi = pltpu.make_async_copy(gtotal.at[:, pl.ds(0, feat)], gin.at[0], lsem.at[2])
    out_go = pltpu.make_async_copy(gtotal.at[:, pl.ds(feat, grouped - feat)], gout.at[0], lsem.at[3])
    out_gi.start()
    out_go.start()
    for made in (out_tg, out_pj, out_gi, out_go):
        made.wait()
    for made in sent:
        made.wait_send()


def finish(*refs):
    n = 4
    writes = [pltpu.make_async_copy(refs[i], refs[n + i], refs[2 * n].at[i]) for i in range(n)]
    for made in writes:
        made.start()
    for made in writes:
        made.wait()


COPIES = 128


def shards(tok, w, cot, ain, aout, tenant, storage):
    rows, feat = tok.shape
    cols = cot.shape[1]
    rank = ain.shape[1]
    nb = tenant.shape[0]
    grouped = feat + cols
    smem = pl.BlockSpec(memory_space=pltpu.SMEM)
    anywhere = pl.BlockSpec(memory_space=pl.ANY)
    shapes = ((rows, cols), (rows, feat), ain.shape, aout.shape)
    results = pl.pallas_call(
        kernel,
        out_shape=tuple(jax.ShapeDtypeStruct(shape, F32) for shape in shapes),
        in_specs=[smem, smem] + [anywhere] * 5,
        out_specs=[anywhere] * 4,
        scratch_shapes=[
            pltpu.VMEM((rows, feat), BF16),
            pltpu.VMEM(w.shape, BF16),
            pltpu.VMEM((rows, cols), BF16),
            pltpu.VMEM((rows, feat), F32),
            pltpu.VMEM((rank, grouped), F32),
            pltpu.VMEM((NX * NZ, rank, grouped), BF16),
            pltpu.VMEM((NX, nb, 128), F32),
            pltpu.VMEM((NZ, 1, 128), F32),
            pltpu.VMEM((NY, rows, NC * cols), BF16),
            pltpu.VMEM((rows, feat), BF16),
            pltpu.VMEM((NY, feat, cols), BF16),
            pltpu.VMEM((NY, rows, cols), F32),
            pltpu.VMEM((14, rows // 2 + 16, cols), BF16),
            pltpu.VMEM((7, rows // 2 + 16, cols), BF16),
            pltpu.VMEM((7, rows // 2 + 16, cols), BF16),
            pltpu.VMEM((NT, 8, 128), F32),
            pltpu.VMEM((NT, 8, 128), F32),
            pltpu.VMEM((NT, 8, 128), F32),
            pltpu.VMEM((NX, nb, rank, grouped + 128), BF16),
            pltpu.VMEM((NX * nb, rank, grouped), F32),
            pltpu.VMEM((NZ, rank, grouped + 128), BF16),
            pltpu.VMEM((NZ, rank, grouped + 128), BF16),
            pltpu.SemaphoreType.DMA((COPIES,)),
            pltpu.SemaphoreType.DMA((COPIES,)),
            pltpu.SemaphoreType.DMA((6,)),
        ],
        compiler_params=pltpu.CompilerParams(
            collective_id=0, has_side_effects=True, vmem_limit_bytes=VMEM_GRANT
        ),
    )(tenant, storage, tok, w, cot, ain, aout)
    return pl.pallas_call(
        finish,
        out_shape=tuple(jax.ShapeDtypeStruct(shape, F32) for shape in shapes),
        in_specs=[anywhere] * 4,
        out_specs=[anywhere] * 4,
        scratch_shapes=[pltpu.SemaphoreType.DMA((4,))],
        compiler_params=pltpu.CompilerParams(vmem_limit_bytes=2 * 1024 * 1024),
    )(*results)


VMEM_GRANT = 24 * 1024 * 1024


def solution(mesh):
    placed = (
        P("rep", "tp"),
        P("tp", None),
        P("rep", "tp"),
        P("rep", None, "tp"),
        P("rep", None, "tp"),
        P("rep"),
        P(),
    )
    return jax.shard_map(
        shards,
        mesh=mesh,
        in_specs=placed,
        out_specs=(P("rep", "tp"), P("rep", "tp"), P("rep", None, "tp"), P("rep", None, "tp")),
        check_vma=False,
    )
```

```python
import functools

import jax
import jax.numpy as jnp
from jax import lax
from jax.experimental import pallas as pl
from jax.experimental.pallas import tpu as pltpu
from jax.sharding import PartitionSpec as P

MESH = pl.DeviceIdType.MESH
F32, BF16 = jnp.float32, jnp.bfloat16
NX, NY, NZ, NC = 4, 8, 8, 2
NT = NY * NC
BLOCK = 128
NT_DIMS = (((1,), (1,)), ((), ()))
TN_DIMS = (((0,), (0,)), ((), ()))


def dot(a, b):
    return jnp.dot(a, b, preferred_element_type=F32)


def dot_nt(a, b):
    return lax.dot_general(a, b, NT_DIMS, preferred_element_type=F32)


def dot_tn(a, b):
    return lax.dot_general(a, b, TN_DIMS, preferred_element_type=F32)


def two_parts(v):
    high = v.astype(BF16)
    low = (v - high.astype(F32)).astype(BF16)
    return jnp.concatenate([high, low], axis=0)


def encode(v):
    top = jnp.max(jnp.max(jnp.abs(v), axis=0, keepdims=True), axis=1, keepdims=True)
    e = jnp.floor(jnp.log2(jnp.maximum(top, 1e-30)))
    scale = jnp.exp2(6.0 - e).astype(BF16).astype(F32)
    inverse = jnp.exp2(e - 6.0).astype(BF16).astype(F32)
    u = v * scale
    p = u * u
    p = p * p
    p = p * p
    p = p * p
    return jnp.where(u < 0, -p, p).astype(BF16), inverse


def decode(code, inverse):
    y = code.astype(F32)
    p = lax.rsqrt(lax.rsqrt(lax.rsqrt(lax.rsqrt(jnp.abs(y)))))
    return jnp.where(y < 0, -p, p) * inverse


def encode_grads(v, feat):
    left, linv = encode(v[:, :feat])
    right, rinv = encode(v[:, feat:])
    rank = v.shape[0]
    tail = jnp.concatenate(
        [jnp.broadcast_to(linv, (rank, 64)), jnp.broadcast_to(rinv, (rank, 64))], axis=1
    )
    return jnp.concatenate([left, right, tail.astype(BF16)], axis=1)


def decode_grads(m, feat):
    grouped = m.shape[1] - 128
    linv = m[0:1, grouped:grouped + 1].astype(F32)
    rinv = m[0:1, grouped + 64:grouped + 65].astype(F32)
    return decode(m[:, :feat], linv), decode(m[:, feat:grouped], rinv)


def kernel(
    tenant, storage, tok_in, w_in, cot_in, ain, aout,
    proj, tgrad_out, gin, gout,
    tok, w, cot, tgrad, gtotal,
    maps, sel, cnt, cotf, tokp, wp, base, rs_out, rs_right, rs_left,
    part, part_in, full, gx, gown, gz_out, gz_in,
    ssem, rsem, lsem,
):
    r, t = lax.axis_index("rep"), lax.axis_index("tp")
    z, x = lax.div(r, NX), lax.rem(r, NX)
    y, c = lax.div(t, NC), lax.rem(t, NC)
    rows = tok.shape[0]
    half = rows // 2
    nb = rows // BLOCK
    feat = tok.shape[1]
    rank = ain.shape[1]
    grouped = feat + cot.shape[1]
    other = 1 - c

    def at_y(d):
        return (r, lax.rem(y + d + NY, NY) * NC + c)

    def at_x(d):
        return (z * NX + lax.rem(x + d + NX, NX), t)

    def at_z(d):
        return (lax.rem(z + d + NZ, NZ) * NX + x, t)

    mate = (r, y * NC + other)
    counter = [0]
    sent = []

    def copy_to(src, dst, device):
        i = counter[0]
        counter[0] += 1
        made = pltpu.make_async_remote_copy(
            src_ref=src, dst_ref=dst, send_sem=ssem.at[i], recv_sem=rsem.at[i],
            device_id=device, device_id_type=MESH,
        )
        made.start()
        sent.append(made)
        return made

    own_lanes = pl.ds(pl.multiple_of(c * 128, 128), 128)
    local = [
        pltpu.make_async_copy(ain.at[0], maps.at[r, :, pl.ds(0, feat)], lsem.at[0]),
        pltpu.make_async_copy(aout.at[0], maps.at[r, :, pl.ds(feat, grouped - feat)], lsem.at[1]),
        pltpu.make_async_copy(cot_in, cot, lsem.at[2]),
        pltpu.make_async_copy(cot_in, cotf.at[y, :, own_lanes], lsem.at[3]),
        pltpu.make_async_copy(tok_in, tok, lsem.at[4]),
        pltpu.make_async_copy(w_in, w, lsem.at[5]),
    ]
    for made in local:
        made.start()

    barrier = pltpu.get_barrier_semaphore()
    greeted = [at_z(k) for k in (4, 3, 5, 2, 6, 1, 7)] + [at_x(2), at_x(1), at_x(3)]
    greeted += [(r, lax.rem(t + k, NT)) for k in range(1, NT)]
    for device in greeted:
        pl.semaphore_signal(barrier, inc=1, device_id=device, device_id_type=MESH)
    lane = lax.broadcasted_iota(jnp.int32, (1, 128), 1)
    slots = [storage[tenant[b]] for b in range(nb)]
    for b in range(nb):
        sel[0, b:b + 1, :] = jnp.where(lane == slots[b], 1.0, 0.0).astype(F32)
    pairs = ((4, 3), (5, 2), (6, 1), (7, 0))

    def w_cols(d, cc):
        yy = lax.rem(y + d, NY)
        return pl.ds(pl.multiple_of(yy * (NC * 128) + cc * 128, 128), 128)

    for made in local:
        made.wait()
    for pair in pairs:
        both = dot(tok[...], jnp.concatenate([w[:, w_cols(d, c)] for d in pair], axis=1))
        base[pair[0]] = both[:, :128]
        base[pair[1]] = both[:, 128:]
    pl.semaphore_wait(barrier, len(greeted))

    maps_z = {k: copy_to(maps.at[r], maps.at[r], at_z(k)) for k in (1, 7, 2, 6, 3, 5, 4)}
    maps_x = [copy_to(maps.at[r], maps.at[r], at_x(k)) for k in (2, 1, 3)]

    def cot_at(yy, cc, lo, size):
        return cotf.at[yy, pl.ds(lo, size), pl.ds(pl.multiple_of(cc * 128, 128), 128)]

    ag_right, ag_left, ag_mate = {}, {}, []
    ag_right[1] = copy_to(cot, cot_at(y, c, 0, rows), at_y(1))
    ag_left[1] = copy_to(cot, cot_at(y, c, 0, rows), at_y(-1))
    tok_mate = copy_to(tok, tokp, mate)
    w_mate = {}

    for d in (4, 3, 5, 2, 6, 1, 7, 0):
        w_mate[d] = copy_to(w.at[:, w_cols(d, other)], wp.at[d], mate)
    ag_mate.append(copy_to(cot, cot_at(y, c, 0, rows), mate))
    sel_x = [copy_to(sel.at[0], sel.at[k], at_x(k)) for k in (1, 2, 3)]

    def mate_pair(pair):
        for d in pair:
            w_mate[d].wait_recv()
        both = dot(tokp[...], jnp.concatenate([wp[d] for d in pair], axis=1))
        base[pair[0]] += both[:, :128]
        base[pair[1]] += both[:, 128:]

    def maps_on(*ks):
        for k in ks:
            maps_z[k].wait_recv()
            came = maps.at[lax.rem(z - k + NZ, NZ) * NX + x]
            for j in (2, 1, 3):
                maps_x.append(copy_to(came, came, at_x(j)))

    def ag_step(s):
        ag_right[s].wait_recv()
        ag_left[s].wait_recv()
        lo_y, hi_y = lax.rem(y - s + NY, NY), lax.rem(y + s, NY)
        size = rows if s < 3 else half
        piece = cot_at(lo_y, c, 0, size)
        ag_right[s + 1] = copy_to(piece, piece, at_y(1))
        piece = cot_at(hi_y, c, rows - size, size)
        ag_left[s + 1] = copy_to(piece, piece, at_y(-1))
        for yy in (lo_y, hi_y):
            piece = cot_at(yy, c, 0, rows)
            ag_mate.append(copy_to(piece, piece, mate))

    rs = {}

    def rs_rows(h):
        return pl.ds(0 if h == "A" else half, half)

    def rs_send(way, h, d):
        slot = len([k for k in rs if k[0] == way])
        target = rs_right if way > 0 else rs_left
        place = slot + (7 if way < 0 else 0)
        code, inverse = encode(base[(way * d) % NY, rs_rows(h), :])
        rs_out[place, :half, :] = code
        rs_out[place, half:, :] = jnp.broadcast_to(inverse, (16, 128)).astype(BF16)
        made = copy_to(rs_out.at[place], target.at[slot], at_y(way))
        rs[way, h, d] = (made, slot)

    def rs_take(way, h, d):
        made, slot = rs[way, h, d]
        made.wait_recv()
        source = rs_right if way > 0 else rs_left
        inverse = source[slot, half:half + 1, :].astype(F32)
        base[(way * (d - 1)) % NY, rs_rows(h), :] += decode(source[slot, :half, :], inverse)

    def rs_hop(d, first):
        right, left = ("A", "B") if first else ("B", "A")
        rs_take(1, right, d + 1)
        rs_send(1, right, d)
        rs_take(-1, left, d + 1)
        rs_send(-1, left, d)

    def through(yy):
        tgrad[...] += dot_nt(cotf[yy], w[:, pl.ds(pl.multiple_of(yy * 256, 256), 256)])

    def through_steps(*pieces):
        for i, s in pieces:
            ag_mate[i].wait_recv()
            through(lax.rem(y - s + NY, NY))

    tok_mate.wait_recv()
    mate_pair(pairs[0])
    rs_send(1, "A", 4)
    rs_send(-1, "B", 4)
    rs_send(1, "B", 3)
    maps_on(1, 7)
    mate_pair(pairs[1])
    rs_send(-1, "A", 3)
    maps_on(2, 6)
    ag_step(1)
    mate_pair(pairs[2])
    maps_on(3, 5)
    mate_pair(pairs[3])
    maps_on(4)
    rs_hop(3, True)
    ag_step(2)
    rs_hop(2, False)
    for made in sel_x:
        made.wait_recv()
    cnt[0] = jnp.sum(jnp.sum(sel[...], axis=0), axis=0, keepdims=True)
    counted = [copy_to(cnt.at[0], cnt.at[k], at_z(k)) for k in range(1, NZ)]
    rs_hop(2, True)

    for made in maps_x:
        made.wait_recv()
    chosen = [maps[slots[b]] for b in range(nb)]
    for b in range(0, nb, 2):
        here = pl.ds(b * BLOCK, 2 * BLOCK)
        two = jnp.concatenate([chosen[b], chosen[b + 1]], axis=0)
        pin = dot_nt(two[:, :feat], tok[here, :])
        pback = dot_nt(two[:, feat:], cot[here, :])
        for i in range(2):
            mine = slice(i * BLOCK, (i + 1) * BLOCK)
            part[b + i] = pin[rank * i:rank * i + 8, mine]
            part[nb + b + i] = pin[rank * i + 8:rank * i + 16, mine]
            part[2 * nb + b + i] = pback[rank * i:rank * i + 8, mine]
            part[3 * nb + b + i] = pback[rank * i + 8:rank * i + 16, mine]

    sums = []
    for k in (8, 7, 9, 6, 10, 5, 11, 4, 12, 3, 13, 2, 14, 1, 15):
        tt = lax.rem(t + k, NT)
        sums.append(copy_to(part.at[tt], part_in.at[k], (r, tt)))

    ag_step(3)
    rs_hop(1, False)
    ag_mate[0].wait_recv()
    tgrad[...] = dot_nt(cotf[y], w[:, pl.ds(pl.multiple_of(y * 256, 256), 256)])
    through_steps((1, 1))

    total = part[t]
    for made in sums:
        made.wait_recv()
    for k in range(1, NT):
        total = total + part_in[k]
    full[t] = total
    spread = []
    for k in (8, 7, 9, 6, 10, 5, 11, 4, 12, 3, 13, 2, 14, 1, 15):
        spread.append(copy_to(full.at[t], full.at[t], (r, lax.rem(t + k, NT))))

    rs_hop(1, True)
    ag_right[4].wait_recv()
    ag_left[4].wait_recv()
    far = cot_at(lax.rem(y + 4, NY), c, 0, rows)
    ag_mate.append(copy_to(far, far, mate))
    through_steps((2, -1), (3, 2), (4, -2))

    for made in spread:
        made.wait_recv()
    rin = [two_parts(jnp.concatenate([full[b], full[nb + b]], axis=0)) for b in range(nb)]
    rback = [two_parts(jnp.concatenate([full[2 * nb + b], full[3 * nb + b]], axis=0)) for b in range(nb)]
    for b in range(nb):
        here = pl.ds(b * BLOCK, BLOCK)
        da = dot(rback[b], tok[here, :])
        db = dot(rin[b], cot[here, :])
        own = jnp.concatenate([da[:rank] + da[rank:], db[:rank] + db[rank:]], axis=1)
        gown[b] = own
        gx[0, b] = encode_grads(own, feat)
    grads_x = [copy_to(gx.at[0], gx.at[k], at_x(k)) for k in (2, 1, 3)]

    for b in range(nb):
        here = pl.ds(b * BLOCK, BLOCK)
        amap = jnp.concatenate([chosen[b][:, :feat]] * 2, axis=0)
        bmap = jnp.concatenate([chosen[b][:, feat:]] * 2, axis=0)
        tgrad[here, :] += 2.0 * dot_tn(rback[b], amap)
        base[0, here, :] += 2.0 * dot_tn(rin[b], bmap)
    through_steps((5, 3), (6, -3))

    for made in grads_x:
        made.wait_recv()
    for k in range(1, NX):
        for b in range(nb):
            one, two = decode_grads(gx[k, b], feat)
            gown[k * nb + b, :, :feat] = one
            gown[k * nb + b, :, feat:] = two
    grads_z = {}
    for d in (4, 3, 5, 2, 6, 1, 7, 0):
        owner = lax.rem(z + d, NZ) * NX + x
        acc = jnp.zeros((rank, grouped), F32)
        for k in range(NX):
            weight = jnp.sum(jnp.where(lane == owner, sel[k], 0.0), axis=1, keepdims=True)
            for b in range(nb):
                acc = acc + weight[b:b + 1, :] * gown[k * nb + b]
        if d:
            gz_out[d] = encode_grads(acc, feat)
            grads_z[d] = copy_to(gz_out.at[d], gz_in.at[d], at_z(d))
        else:
            gtotal[...] = acc

    through_steps((7, 4))
    out_tg = pltpu.make_async_copy(tgrad, tgrad_out, lsem.at[0])
    out_tg.start()

    rs_take(1, "B", 1)
    rs_take(-1, "A", 1)
    rs_take(1, "A", 1)
    rs_take(-1, "B", 1)
    out_pj = pltpu.make_async_copy(base.at[0], proj, lsem.at[1])
    out_pj.start()

    for made in counted:
        made.wait_recv()
    blocks_of = jnp.sum(cnt[...], axis=0)
    mine = jnp.sum(jnp.where(lane == r, blocks_of, 0.0), axis=1, keepdims=True)
    scale = 2.0 / jnp.maximum(mine * float(BLOCK), 1.0)
    acc_in, acc_out = gtotal[:, :feat], gtotal[:, feat:]
    for d in (1, 7, 2, 6, 3, 5, 4):
        grads_z[d].wait_recv()
        one, two = decode_grads(gz_in[d], feat)
        acc_in, acc_out = acc_in + one, acc_out + two
    gtotal[:, :feat] = acc_in * scale
    gtotal[:, feat:] = acc_out * scale
    out_gi = pltpu.make_async_copy(gtotal.at[:, pl.ds(0, feat)], gin.at[0], lsem.at[2])
    out_go = pltpu.make_async_copy(gtotal.at[:, pl.ds(feat, grouped - feat)], gout.at[0], lsem.at[3])
    out_gi.start()
    out_go.start()
    for made in (out_tg, out_pj, out_gi, out_go):
        made.wait()
    for made in sent:
        made.wait_send()


def finish(*refs):
    n = 4
    sources, targets, held, came, gone = refs[:n], refs[n:2 * n], refs[2 * n:3 * n], refs[3 * n], refs[3 * n + 1]
    reads = [pltpu.make_async_copy(sources[i], held[i], came.at[i]) for i in range(n)]
    writes = [pltpu.make_async_copy(held[i], targets[i], gone.at[i]) for i in range(n)]
    for made in reads:
        made.start()
    for i in range(n):
        reads[i].wait()
        writes[i].start()
    for made in writes:
        made.wait()


COPIES = 128


def shards(tok, w, cot, ain, aout, tenant, storage):
    rows, feat = tok.shape
    cols = cot.shape[1]
    rank = ain.shape[1]
    nb = tenant.shape[0]
    grouped = feat + cols
    smem = pl.BlockSpec(memory_space=pltpu.SMEM)
    anywhere = pl.BlockSpec(memory_space=pl.ANY)
    shapes = ((rows, cols), (rows, feat), ain.shape, aout.shape)
    results = pl.pallas_call(
        kernel,
        out_shape=tuple(jax.ShapeDtypeStruct(shape, F32) for shape in shapes),
        in_specs=[smem, smem] + [anywhere] * 5,
        out_specs=[anywhere] * 4,
        scratch_shapes=[
            pltpu.VMEM((rows, feat), BF16),
            pltpu.VMEM(w.shape, BF16),
            pltpu.VMEM((rows, cols), BF16),
            pltpu.VMEM((rows, feat), F32),
            pltpu.VMEM((rank, grouped), F32),
            pltpu.VMEM((NX * NZ, rank, grouped), BF16),
            pltpu.VMEM((NX, nb, 128), F32),
            pltpu.VMEM((NZ, 1, 128), F32),
            pltpu.VMEM((NY, rows, NC * cols), BF16),
            pltpu.VMEM((rows, feat), BF16),
            pltpu.VMEM((NY, feat, cols), BF16),
            pltpu.VMEM((NY, rows, cols), F32),
            pltpu.VMEM((14, rows // 2 + 16, cols), BF16),
            pltpu.VMEM((7, rows // 2 + 16, cols), BF16),
            pltpu.VMEM((7, rows // 2 + 16, cols), BF16),
            pltpu.VMEM((NT, 8, 128), F32),
            pltpu.VMEM((NT, 8, 128), F32),
            pltpu.VMEM((NT, 8, 128), F32),
            pltpu.VMEM((NX, nb, rank, grouped + 128), BF16),
            pltpu.VMEM((NX * nb, rank, grouped), F32),
            pltpu.VMEM((NZ, rank, grouped + 128), BF16),
            pltpu.VMEM((NZ, rank, grouped + 128), BF16),
            pltpu.SemaphoreType.DMA((COPIES,)),
            pltpu.SemaphoreType.DMA((COPIES,)),
            pltpu.SemaphoreType.DMA((6,)),
        ],
        compiler_params=pltpu.CompilerParams(
            collective_id=0, has_side_effects=True, vmem_limit_bytes=VMEM_GRANT
        ),
    )(tenant, storage, tok, w, cot, ain, aout)
    return pl.pallas_call(
        finish,
        out_shape=tuple(jax.ShapeDtypeStruct(shape, F32) for shape in shapes),
        in_specs=[anywhere] * 4,
        out_specs=[anywhere] * 4,
        scratch_shapes=[pltpu.VMEM(shape, F32) for shape in shapes]
        + [pltpu.SemaphoreType.DMA((4,)), pltpu.SemaphoreType.DMA((4,))],
        compiler_params=pltpu.CompilerParams(vmem_limit_bytes=VMEM_GRANT),
    )(*results)


VMEM_GRANT = 63 * 1024 * 1024


def solution(mesh):
    placed = (
        P("rep", "tp"),
        P("tp", None),
        P("rep", "tp"),
        P("rep", None, "tp"),
        P("rep", None, "tp"),
        P("rep"),
        P(),
    )
    return jax.shard_map(
        shards,
        mesh=mesh,
        in_specs=placed,
        out_specs=(P("rep", "tp"), P("rep", "tp"), P("rep", None, "tp"), P("rep", None, "tp")),
        check_vma=False,
    )
```

```python
import functools

import jax
import jax.numpy as jnp
from jax import lax
from jax.experimental import pallas as pl
from jax.experimental.pallas import tpu as pltpu
from jax.sharding import PartitionSpec as P

MESH = pl.DeviceIdType.MESH
F32, BF16 = jnp.float32, jnp.bfloat16
NX, NY, NZ, NC = 4, 8, 8, 2
NT = NY * NC
BLOCK = 128
NT_DIMS = (((1,), (1,)), ((), ()))
TN_DIMS = (((0,), (0,)), ((), ()))


def dot(a, b):
    return jnp.dot(a, b, preferred_element_type=F32)


def dot_nt(a, b):
    return lax.dot_general(a, b, NT_DIMS, preferred_element_type=F32)


def dot_tn(a, b):
    return lax.dot_general(a, b, TN_DIMS, preferred_element_type=F32)


def two_parts(v):
    high = v.astype(BF16)
    low = (v - high.astype(F32)).astype(BF16)
    return jnp.concatenate([high, low], axis=0)


def encode(v):
    top = jnp.max(jnp.max(jnp.abs(v), axis=0, keepdims=True), axis=1, keepdims=True)
    e = jnp.floor(jnp.log2(jnp.maximum(top, 1e-30)))
    scale = jnp.exp2(6.0 - e).astype(BF16).astype(F32)
    inverse = jnp.exp2(e - 6.0).astype(BF16).astype(F32)
    u = v * scale
    p = u * u
    p = p * p
    p = p * p
    p = p * p
    return jnp.where(u < 0, -p, p).astype(BF16), inverse


def decode(code, inverse):
    y = code.astype(F32)
    p = lax.rsqrt(lax.rsqrt(lax.rsqrt(lax.rsqrt(jnp.abs(y)))))
    return jnp.where(y < 0, -p, p) * inverse


def encode_wide(v):
    code, inverse = encode(v)
    tail = jnp.broadcast_to(inverse, (v.shape[0], 128)).astype(BF16)
    return jnp.concatenate([code, tail], axis=1)


def decode_wide(m):
    n = m.shape[1] - 128
    return decode(m[:, :n], m[0:1, n:n + 1].astype(F32))


def kernel(
    tenant, storage, tok_in, w_in, cot_in, ain, aout,
    proj, tgrad_out, gin, gout,
    tok, w, cot, tgrad, gtotal,
    maps_a, maps_b, sel, cnt, cotf, tokp, wp, base, rs_out, rs_right, rs_left,
    part, part_in, full, gxa, gxb, owna, ownb, za_out, zb_out, za_in, zb_in,
    ssem, rsem, lsem,
):
    r, t = lax.axis_index("rep"), lax.axis_index("tp")
    z, x = lax.div(r, NX), lax.rem(r, NX)
    y, c = lax.div(t, NC), lax.rem(t, NC)
    rows = tok.shape[0]
    half = rows // 2
    nb = rows // BLOCK
    feat = tok.shape[1]
    rank = ain.shape[1]
    grouped = feat + cot.shape[1]
    other = 1 - c

    def at_y(d):
        return (r, lax.rem(y + d + NY, NY) * NC + c)

    def at_x(d):
        return (z * NX + lax.rem(x + d + NX, NX), t)

    def at_z(d):
        return (lax.rem(z + d + NZ, NZ) * NX + x, t)

    mate = (r, y * NC + other)
    counter = [0]
    sent = []

    def copy_to(src, dst, device):
        i = counter[0]
        counter[0] += 1
        made = pltpu.make_async_remote_copy(
            src_ref=src, dst_ref=dst, send_sem=ssem.at[i], recv_sem=rsem.at[i],
            device_id=device, device_id_type=MESH,
        )
        made.start()
        sent.append(made)
        return made

    own_lanes = pl.ds(pl.multiple_of(c * 128, 128), 128)
    local = [
        pltpu.make_async_copy(ain.at[0], maps_a.at[r], lsem.at[0]),
        pltpu.make_async_copy(aout.at[0], maps_b.at[r], lsem.at[1]),
        pltpu.make_async_copy(cot_in, cot, lsem.at[2]),
        pltpu.make_async_copy(cot_in, cotf.at[y, :, own_lanes], lsem.at[3]),
        pltpu.make_async_copy(tok_in, tok, lsem.at[4]),
        pltpu.make_async_copy(w_in, w, lsem.at[5]),
    ]
    for made in local:
        made.start()

    barrier = pltpu.get_barrier_semaphore()
    greeted = [at_z(k) for k in (4, 3, 5, 2, 6, 1, 7)] + [at_x(2), at_x(1), at_x(3)]
    greeted += [(r, lax.rem(t + k, NT)) for k in range(1, NT)]
    for device in greeted:
        pl.semaphore_signal(barrier, inc=1, device_id=device, device_id_type=MESH)
    lane = lax.broadcasted_iota(jnp.int32, (1, 128), 1)
    slots = [storage[tenant[b]] for b in range(nb)]
    for b in range(nb):
        sel[0, b:b + 1, :] = jnp.where(lane == slots[b], 1.0, 0.0).astype(F32)
    pairs = ((4, 3), (5, 2), (6, 1), (7, 0))

    def w_cols(d, cc):
        yy = lax.rem(y + d, NY)
        return pl.ds(pl.multiple_of(yy * (NC * 128) + cc * 128, 128), 128)

    for made in local[:4]:
        made.wait()
    pl.semaphore_wait(barrier, len(greeted))

    near_z, near_x = (1, 7, 2, 6, 3, 5, 4), (2, 1, 3)
    along_z, along_x = {}, {}
    for kind, maps in (("b", maps_b), ("a", maps_a)):
        for k in near_z:
            along_z[kind, k] = copy_to(maps.at[r], maps.at[r], at_z(k))
        along_x[kind] = [copy_to(maps.at[r], maps.at[r], at_x(k)) for k in near_x]

    def cot_at(yy, cc, lo, size):
        return cotf.at[yy, pl.ds(lo, size), pl.ds(pl.multiple_of(cc * 128, 128), 128)]

    ag_right, ag_left, ag_mate = {}, {}, []
    ag_right[1] = copy_to(cot, cot_at(y, c, 0, rows), at_y(1))
    ag_left[1] = copy_to(cot, cot_at(y, c, 0, rows), at_y(-1))
    for made in local[4:]:
        made.wait()
    tok_mate = copy_to(tok, tokp, mate)
    w_mate = {}

    for d in (4, 3, 5, 2, 6, 1, 7, 0):
        w_mate[d] = copy_to(w.at[:, w_cols(d, other)], wp.at[d], mate)
    ag_mate.append(copy_to(cot, cot_at(y, c, 0, rows), mate))
    sel_x = [copy_to(sel.at[0], sel.at[k], at_x(k)) for k in (1, 2, 3)]

    def mate_pair(pair):
        for d in pair:
            w_mate[d].wait_recv()
        both = dot(tokp[...], jnp.concatenate([wp[d] for d in pair], axis=1))
        base[pair[0]] += both[:, :128]
        base[pair[1]] += both[:, 128:]

    def own_pair(pair):
        both = dot(tok[...], jnp.concatenate([w[:, w_cols(d, c)] for d in pair], axis=1))
        base[pair[0]] = both[:, :128]
        base[pair[1]] = both[:, 128:]

    def maps_on(kind, *ks):
        maps = maps_a if kind == "a" else maps_b
        for k in ks:
            along_z[kind, k].wait_recv()
            came = maps.at[lax.rem(z - k + NZ, NZ) * NX + x]
            for j in near_x:
                along_x[kind].append(copy_to(came, came, at_x(j)))

    def blocks_of(i):
        return pl.ds(i * BLOCK, BLOCK)

    far_first = (8, 7, 9, 6, 10, 5, 11, 4, 12, 3, 13, 2, 14, 1, 15)
    sums, spread = {}, {}

    def rank_start(i, kind, maps, data):
        for made in along_x[kind]:
            made.wait_recv()
        chosen = [maps[slots[b]] for b in range(nb)]
        for b in range(0, nb, 2):
            two = jnp.concatenate([chosen[b], chosen[b + 1]], axis=0)
            both = dot_nt(two, data[pl.ds(b * BLOCK, 2 * BLOCK), :])
            for h in range(2):
                for j in range(4):
                    lo = rank * h + 4 * j
                    part[i, j * nb + b + h] = both[lo:lo + 4, h * BLOCK:(h + 1) * BLOCK]
        sums[i] = []
        for k in far_first:
            tt = lax.rem(t + k, NT)
            sums[i].append(copy_to(part.at[i, tt], part_in.at[i, k], (r, tt)))
        return chosen

    def rank_middle(i):
        total = part[i, t]
        for made in sums[i]:
            made.wait_recv()
        for k in range(1, NT):
            total = total + part_in[i, k]
        full[i, t] = total
        spread[i] = [copy_to(full.at[i, t], full.at[i, t], (r, lax.rem(t + k, NT))) for k in far_first]

    def rank_end(i):
        for made in spread[i]:
            made.wait_recv()
        return [
            two_parts(jnp.concatenate([full[i, j * nb + b] for j in range(4)], axis=0))
            for b in range(nb)
        ]

    def grads_start(ranks, data, gx, own):
        for b in range(nb):
            g = dot(ranks[b], data[blocks_of(b), :])
            g = g[:rank] + g[rank:]
            own[b] = g
            gx[0, b] = encode_wide(g)
        return [copy_to(gx.at[0], gx.at[k], at_x(k)) for k in near_x]

    def grads_middle(going, gx, own, out, into, lo):
        for made in going:
            made.wait_recv()
        for k in range(1, NX):
            for b in range(nb):
                own[k * nb + b] = decode_wide(gx[k, b])
        made = {}
        n = own.shape[2]
        for d in near_z + (0,):
            owner = lax.rem(z + d, NZ) * NX + x
            acc = jnp.zeros((rank, n), F32)
            for k in range(NX):
                weight = jnp.sum(jnp.where(lane == owner, sel[k], 0.0), axis=1, keepdims=True)
                for b in range(nb):
                    acc = acc + weight[b:b + 1, :] * own[k * nb + b]
            if d:
                out[d] = encode_wide(acc)
                made[d] = copy_to(out.at[d], into.at[d], at_z(d))
            else:
                gtotal[:, lo:lo + n] = acc
        return made

    def grads_end(going, into, lo, n, scale):
        acc = gtotal[:, lo:lo + n]
        for d in near_z:
            going[d].wait_recv()
            acc = acc + decode_wide(into[d])
        gtotal[:, lo:lo + n] = acc * scale

    def ag_step(s):
        ag_right[s].wait_recv()
        ag_left[s].wait_recv()
        lo_y, hi_y = lax.rem(y - s + NY, NY), lax.rem(y + s, NY)
        size = rows if s < 3 else half
        piece = cot_at(lo_y, c, 0, size)
        ag_right[s + 1] = copy_to(piece, piece, at_y(1))
        piece = cot_at(hi_y, c, rows - size, size)
        ag_left[s + 1] = copy_to(piece, piece, at_y(-1))
        for yy in (lo_y, hi_y):
            piece = cot_at(yy, c, 0, rows)
            ag_mate.append(copy_to(piece, piece, mate))

    rs = {}

    def rs_rows(h):
        return pl.ds(0 if h == "A" else half, half)

    def rs_send(way, h, d):
        slot = len([k for k in rs if k[0] == way])
        target = rs_right if way > 0 else rs_left
        place = slot + (7 if way < 0 else 0)
        code, inverse = encode(base[(way * d) % NY, rs_rows(h), :])
        rs_out[place, :half, :] = code
        rs_out[place, half:, :] = jnp.broadcast_to(inverse, (16, 128)).astype(BF16)
        made = copy_to(rs_out.at[place], target.at[slot], at_y(way))
        rs[way, h, d] = (made, slot)

    def rs_take(way, h, d):
        made, slot = rs[way, h, d]
        made.wait_recv()
        source = rs_right if way > 0 else rs_left
        inverse = source[slot, half:half + 1, :].astype(F32)
        base[(way * (d - 1)) % NY, rs_rows(h), :] += decode(source[slot, :half, :], inverse)

    def rs_hop(d, first):
        right, left = ("A", "B") if first else ("B", "A")
        rs_take(1, right, d + 1)
        rs_send(1, right, d)
        rs_take(-1, left, d + 1)
        rs_send(-1, left, d)

    def through(yy):
        tgrad[...] += dot_nt(cotf[yy], w[:, pl.ds(pl.multiple_of(yy * 256, 256), 256)])

    def through_steps(*pieces):
        for i, s in pieces:
            ag_mate[i].wait_recv()
            through(lax.rem(y - s + NY, NY))

    maps_on("b", 1, 7)
    own_pair(pairs[0])
    maps_on("b", 2, 6)
    maps_on("a", 1, 7)
    own_pair(pairs[1])
    tok_mate.wait_recv()
    mate_pair(pairs[0])
    rs_send(1, "A", 4)
    rs_send(-1, "B", 4)
    maps_on("b", 3, 5)
    maps_on("a", 2, 6)
    maps_on("b", 4)
    rs_send(1, "B", 3)
    mate_pair(pairs[1])
    rs_send(-1, "A", 3)
    ag_step(1)
    maps_on("a", 3, 5)
    maps_on("a", 4)
    chosen_b = rank_start(0, "b", maps_b, cot)
    own_pair(pairs[2])
    own_pair(pairs[3])
    mate_pair(pairs[2])
    rs_hop(3, True)
    ag_step(2)
    chosen_a = rank_start(1, "a", maps_a, tok)
    rank_middle(0)
    mate_pair(pairs[3])
    rs_hop(2, False)
    for made in sel_x:
        made.wait_recv()
    cnt[0] = jnp.sum(jnp.sum(sel[...], axis=0), axis=0, keepdims=True)
    counted = [copy_to(cnt.at[0], cnt.at[k], at_z(k)) for k in range(1, NZ)]
    rs_hop(2, True)
    ag_step(3)
    rank_middle(1)
    rback = rank_end(0)
    going_a = grads_start(rback, tok, gxa, owna)
    rs_hop(1, False)
    ag_mate[0].wait_recv()
    tgrad[...] = dot_nt(cotf[y], w[:, pl.ds(pl.multiple_of(y * 256, 256), 256)])
    through_steps((1, 1))
    rin = rank_end(1)
    going_b = grads_start(rin, cot, gxb, ownb)
    rs_hop(1, True)
    ag_right[4].wait_recv()
    ag_left[4].wait_recv()
    far = cot_at(lax.rem(y + 4, NY), c, 0, rows)
    ag_mate.append(copy_to(far, far, mate))
    going_a = grads_middle(going_a, gxa, owna, za_out, za_in, 0)
    through_steps((2, -1))
    going_b = grads_middle(going_b, gxb, ownb, zb_out, zb_in, feat)
    for b in range(nb):
        here = blocks_of(b)
        tgrad[here, :] += 2.0 * dot_tn(rback[b], jnp.concatenate([chosen_a[b]] * 2, axis=0))
        base[0, here, :] += 2.0 * dot_tn(rin[b], jnp.concatenate([chosen_b[b]] * 2, axis=0))
    rs_take(1, "B", 1)
    rs_take(-1, "A", 1)
    rs_take(1, "A", 1)
    rs_take(-1, "B", 1)
    out_pj = pltpu.make_async_copy(base.at[0], proj, lsem.at[1])
    out_pj.start()
    through_steps((3, 2), (4, -2), (5, 3), (6, -3), (7, 4))
    out_tg = pltpu.make_async_copy(tgrad, tgrad_out, lsem.at[0])
    out_tg.start()

    for made in counted:
        made.wait_recv()
    all_counts = jnp.sum(cnt[...], axis=0)
    mine = jnp.sum(jnp.where(lane == r, all_counts, 0.0), axis=1, keepdims=True)
    scale = 2.0 / jnp.maximum(mine * float(BLOCK), 1.0)
    grads_end(going_a, za_in, 0, feat, scale)
    grads_end(going_b, zb_in, feat, grouped - feat, scale)
    out_gi = pltpu.make_async_copy(gtotal.at[:, pl.ds(0, feat)], gin.at[0], lsem.at[2])
    out_go = pltpu.make_async_copy(gtotal.at[:, pl.ds(feat, grouped - feat)], gout.at[0], lsem.at[3])
    out_gi.start()
    out_go.start()
    for made in (out_tg, out_pj, out_gi, out_go):
        made.wait()
    for made in sent:
        made.wait_send()


def finish(*refs):
    n = 4
    sources, targets, held, came, gone = refs[:n], refs[n:2 * n], refs[2 * n:3 * n], refs[3 * n], refs[3 * n + 1]
    reads = [pltpu.make_async_copy(sources[i], held[i], came.at[i]) for i in range(n)]
    writes = [pltpu.make_async_copy(held[i], targets[i], gone.at[i]) for i in range(n)]
    for made in reads:
        made.start()
    for i in range(n):
        reads[i].wait()
        writes[i].start()
    for made in writes:
        made.wait()


COPIES = 224


def shards(tok, w, cot, ain, aout, tenant, storage):
    rows, feat = tok.shape
    cols = cot.shape[1]
    rank = ain.shape[1]
    nb = tenant.shape[0]
    grouped = feat + cols
    smem = pl.BlockSpec(memory_space=pltpu.SMEM)
    anywhere = pl.BlockSpec(memory_space=pl.ANY)
    shapes = ((rows, cols), (rows, feat), ain.shape, aout.shape)
    results = pl.pallas_call(
        kernel,
        out_shape=tuple(jax.ShapeDtypeStruct(shape, F32) for shape in shapes),
        in_specs=[smem, smem] + [anywhere] * 5,
        out_specs=[anywhere] * 4,
        scratch_shapes=[
            pltpu.VMEM((rows, feat), BF16),
            pltpu.VMEM(w.shape, BF16),
            pltpu.VMEM((rows, cols), BF16),
            pltpu.VMEM((rows, feat), F32),
            pltpu.VMEM((rank, grouped), F32),
            pltpu.VMEM((NX * NZ, rank, feat), BF16),
            pltpu.VMEM((NX * NZ, rank, cols), BF16),
            pltpu.VMEM((NX, nb, 128), F32),
            pltpu.VMEM((NZ, 1, 128), F32),
            pltpu.VMEM((NY, rows, NC * cols), BF16),
            pltpu.VMEM((rows, feat), BF16),
            pltpu.VMEM((NY, feat, cols), BF16),
            pltpu.VMEM((NY, rows, cols), F32),
            pltpu.VMEM((14, rows // 2 + 16, cols), BF16),
            pltpu.VMEM((7, rows // 2 + 16, cols), BF16),
            pltpu.VMEM((7, rows // 2 + 16, cols), BF16),
            pltpu.VMEM((2, NT, 4, 128), F32),
            pltpu.VMEM((2, NT, 4, 128), F32),
            pltpu.VMEM((2, NT, 4, 128), F32),
            pltpu.VMEM((NX, nb, rank, feat + 128), BF16),
            pltpu.VMEM((NX, nb, rank, cols + 128), BF16),
            pltpu.VMEM((NX * nb, rank, feat), F32),
            pltpu.VMEM((NX * nb, rank, cols), F32),
            pltpu.VMEM((NZ, rank, feat + 128), BF16),
            pltpu.VMEM((NZ, rank, cols + 128), BF16),
            pltpu.VMEM((NZ, rank, feat + 128), BF16),
            pltpu.VMEM((NZ, rank, cols + 128), BF16),
            pltpu.SemaphoreType.DMA((COPIES,)),
            pltpu.SemaphoreType.DMA((COPIES,)),
            pltpu.SemaphoreType.DMA((6,)),
        ],
        compiler_params=pltpu.CompilerParams(
            collective_id=0, has_side_effects=True, vmem_limit_bytes=VMEM_GRANT
        ),
    )(tenant, storage, tok, w, cot, ain, aout)
    return pl.pallas_call(
        finish,
        out_shape=tuple(jax.ShapeDtypeStruct(shape, F32) for shape in shapes),
        in_specs=[anywhere] * 4,
        out_specs=[anywhere] * 4,
        scratch_shapes=[pltpu.VMEM(shape, F32) for shape in shapes]
        + [pltpu.SemaphoreType.DMA((4,)), pltpu.SemaphoreType.DMA((4,))],
        compiler_params=pltpu.CompilerParams(vmem_limit_bytes=VMEM_GRANT),
    )(*results)


VMEM_GRANT = 63 * 1024 * 1024


def solution(mesh):
    placed = (
        P("rep", "tp"),
        P("tp", None),
        P("rep", "tp"),
        P("rep", None, "tp"),
        P("rep", None, "tp"),
        P("rep"),
        P(),
    )
    return jax.shard_map(
        shards,
        mesh=mesh,
        in_specs=placed,
        out_specs=(P("rep", "tp"), P("rep", "tp"), P("rep", None, "tp"), P("rep", None, "tp")),
        check_vma=False,
    )
```

```python
import functools

import jax
import jax.numpy as jnp
from jax import lax
from jax.experimental import pallas as pl
from jax.experimental.pallas import tpu as pltpu
from jax.sharding import PartitionSpec as P

MESH = pl.DeviceIdType.MESH
F32, BF16 = jnp.float32, jnp.bfloat16
NX, NY, NZ, NC = 4, 8, 8, 2
NT = NY * NC
BLOCK = 128
NT_DIMS = (((1,), (1,)), ((), ()))
TN_DIMS = (((0,), (0,)), ((), ()))


def dot(a, b):
    return jnp.dot(a, b, preferred_element_type=F32)


def dot_nt(a, b):
    return lax.dot_general(a, b, NT_DIMS, preferred_element_type=F32)


def dot_tn(a, b):
    return lax.dot_general(a, b, TN_DIMS, preferred_element_type=F32)


def two_parts(v):
    high = v.astype(BF16)
    low = (v - high.astype(F32)).astype(BF16)
    return jnp.concatenate([high, low], axis=0)


def encode(v):
    top = jnp.max(jnp.max(jnp.abs(v), axis=0, keepdims=True), axis=1, keepdims=True)
    e = jnp.floor(jnp.log2(jnp.maximum(top, 1e-30)))
    scale = jnp.exp2(6.0 - e).astype(BF16).astype(F32)
    inverse = jnp.exp2(e - 6.0).astype(BF16).astype(F32)
    u = v * scale
    p = u * u
    p = p * p
    p = p * p
    p = p * p
    return jnp.where(u < 0, -p, p).astype(BF16), inverse


def decode(code, inverse):
    y = code.astype(F32)
    p = lax.rsqrt(lax.rsqrt(lax.rsqrt(lax.rsqrt(jnp.abs(y)))))
    return jnp.where(y < 0, -p, p) * inverse


def encode_wide(v):
    code, inverse = encode(v)
    tail = jnp.broadcast_to(inverse, (v.shape[0], 128)).astype(BF16)
    return jnp.concatenate([code, tail], axis=1)


def decode_wide(m):
    n = m.shape[1] - 128
    return decode(m[:, :n], m[0:1, n:n + 1].astype(F32))


def kernel(
    tenant, storage, tok_in, w_in, cot_in, ain, aout,
    proj, tgrad_out, gin, gout,
    tok, w, cot, tgrad, gtotal,
    maps_a, maps_b, sel, cnt, cotf, tokp, wp, base, rs_out, rs_right, rs_left,
    part, part_in, full, gxa, gxb, owna, ownb, za_out, zb_out, za_in, zb_in,
    ssem, rsem, lsem,
):
    r, t = lax.axis_index("rep"), lax.axis_index("tp")
    z, x = lax.div(r, NX), lax.rem(r, NX)
    y, c = lax.div(t, NC), lax.rem(t, NC)
    rows = tok.shape[0]
    half = rows // 2
    nb = rows // BLOCK
    feat = tok.shape[1]
    rank = ain.shape[1]
    grouped = feat + cot.shape[1]
    other = 1 - c

    def at_y(d):
        return (r, lax.rem(y + d + NY, NY) * NC + c)

    def at_x(d):
        return (z * NX + lax.rem(x + d + NX, NX), t)

    def at_z(d):
        return (lax.rem(z + d + NZ, NZ) * NX + x, t)

    mate = (r, y * NC + other)
    counter = [0]
    sent = []

    def copy_to(src, dst, device):
        i = counter[0]
        counter[0] += 1
        made = pltpu.make_async_remote_copy(
            src_ref=src, dst_ref=dst, send_sem=ssem.at[i], recv_sem=rsem.at[i],
            device_id=device, device_id_type=MESH,
        )
        made.start()
        sent.append(made)
        return made

    own_lanes = pl.ds(pl.multiple_of(c * 128, 128), 128)
    local = [
        pltpu.make_async_copy(ain.at[0], maps_a.at[r], lsem.at[0]),
        pltpu.make_async_copy(aout.at[0], maps_b.at[r], lsem.at[1]),
        pltpu.make_async_copy(cot_in, cot, lsem.at[2]),
        pltpu.make_async_copy(cot_in, cotf.at[y, :, own_lanes], lsem.at[3]),
        pltpu.make_async_copy(tok_in, tok, lsem.at[4]),
        pltpu.make_async_copy(w_in, w, lsem.at[5]),
    ]
    for made in local:
        made.start()

    barrier = pltpu.get_barrier_semaphore()
    greeted = [at_z(k) for k in (4, 3, 5, 2, 6, 1, 7)] + [at_x(2), at_x(1), at_x(3)]
    greeted += [(r, lax.rem(t + k, NT)) for k in range(1, NT)]
    for device in greeted:
        pl.semaphore_signal(barrier, inc=1, device_id=device, device_id_type=MESH)
    lane = lax.broadcasted_iota(jnp.int32, (1, 128), 1)
    slots = [storage[tenant[b]] for b in range(nb)]
    for b in range(nb):
        sel[0, b:b + 1, :] = jnp.where(lane == slots[b], 1.0, 0.0).astype(F32)
    pairs = ((4, 3), (5, 2), (6, 1), (7, 0))

    def w_cols(d, cc):
        yy = lax.rem(y + d, NY)
        return pl.ds(pl.multiple_of(yy * (NC * 128) + cc * 128, 128), 128)

    pl.semaphore_wait(barrier, len(greeted))

    near_z, near_x = (1, 7, 2, 6, 3, 5, 4), (2, 1, 3)
    along_z, along_x = {}, {}
    for kind, own, maps in (("b", aout, maps_b), ("a", ain, maps_a)):
        for k in near_z:
            along_z[kind, k] = copy_to(own.at[0], maps.at[r], at_z(k))
        along_x[kind] = [copy_to(own.at[0], maps.at[r], at_x(k)) for k in near_x]

    def cot_at(yy, cc, lo, size):
        return cotf.at[yy, pl.ds(lo, size), pl.ds(pl.multiple_of(cc * 128, 128), 128)]

    ag_right, ag_left, ag_mate = {}, {}, []
    ag_right[1] = copy_to(cot_in, cot_at(y, c, 0, rows), at_y(1))
    ag_left[1] = copy_to(cot_in, cot_at(y, c, 0, rows), at_y(-1))
    for made in local:
        made.wait()
    tok_mate = copy_to(tok, tokp, mate)
    w_mate = {}

    for d in (4, 3, 5, 2, 6, 1, 7, 0):
        w_mate[d] = copy_to(w.at[:, w_cols(d, other)], wp.at[d], mate)
    ag_mate.append(copy_to(cot_in, cot_at(y, c, 0, rows), mate))
    sel_x = [copy_to(sel.at[0], sel.at[k], at_x(k)) for k in (1, 2, 3)]

    def mate_pair(pair):
        for d in pair:
            w_mate[d].wait_recv()
        both = dot(tokp[...], jnp.concatenate([wp[d] for d in pair], axis=1))
        base[pair[0]] += both[:, :128]
        base[pair[1]] += both[:, 128:]

    def own_pair(pair):
        both = dot(tok[...], jnp.concatenate([w[:, w_cols(d, c)] for d in pair], axis=1))
        base[pair[0]] = both[:, :128]
        base[pair[1]] = both[:, 128:]

    def maps_on(kind, *ks):
        maps = maps_a if kind == "a" else maps_b
        for k in ks:
            along_z[kind, k].wait_recv()
            came = maps.at[lax.rem(z - k + NZ, NZ) * NX + x]
            for j in near_x:
                along_x[kind].append(copy_to(came, came, at_x(j)))

    def blocks_of(i):
        return pl.ds(i * BLOCK, BLOCK)

    far_first = (8, 7, 9, 6, 10, 5, 11, 4, 12, 3, 13, 2, 14, 1, 15)
    sums, spread = {}, {}

    def rank_start(i, kind, maps, data):
        for made in along_x[kind]:
            made.wait_recv()
        chosen = [maps[slots[b]] for b in range(nb)]
        for b in range(0, nb, 2):
            two = jnp.concatenate([chosen[b], chosen[b + 1]], axis=0)
            both = dot_nt(two, data[pl.ds(b * BLOCK, 2 * BLOCK), :])
            for h in range(2):
                for j in range(4):
                    lo = rank * h + 4 * j
                    part[i, j * nb + b + h] = both[lo:lo + 4, h * BLOCK:(h + 1) * BLOCK]
        sums[i] = []
        for k in far_first:
            tt = lax.rem(t + k, NT)
            sums[i].append(copy_to(part.at[i, tt], part_in.at[i, k], (r, tt)))
        return chosen

    def rank_middle(i):
        total = part[i, t]
        for made in sums[i]:
            made.wait_recv()
        for k in range(1, NT):
            total = total + part_in[i, k]
        full[i, t] = total
        spread[i] = [copy_to(full.at[i, t], full.at[i, t], (r, lax.rem(t + k, NT))) for k in far_first]

    def rank_end(i):
        for made in spread[i]:
            made.wait_recv()
        return [
            two_parts(jnp.concatenate([full[i, j * nb + b] for j in range(4)], axis=0))
            for b in range(nb)
        ]

    def grads_start(ranks, data, gx, own):
        for b in range(nb):
            g = dot(ranks[b], data[blocks_of(b), :])
            g = g[:rank] + g[rank:]
            own[b] = g
            gx[0, b] = encode_wide(g)
        return [copy_to(gx.at[0], gx.at[k], at_x(k)) for k in near_x]

    far_z = (4, 3, 5, 2, 6, 1, 7)

    def owner_weights():
        return {
            (d, k): jnp.sum(
                jnp.where(lane == lax.rem(z + d, NZ) * NX + x, sel[k], 0.0), axis=1, keepdims=True
            )
            for d in range(NZ) for k in range(NX)
        }

    def grads_middle(weights, going, gx, own, out, into, lo):
        for made in going:
            made.wait_recv()
        for k in range(1, NX):
            for b in range(nb):
                own[k * nb + b] = decode_wide(gx[k, b])
        made = {}
        n = own.shape[2]
        for d in far_z + (0,):
            acc = jnp.zeros((rank, n), F32)
            for k in range(NX):
                for b in range(nb):
                    acc = acc + weights[d, k][b:b + 1, :] * own[k * nb + b]
            if d:
                out[d] = encode_wide(acc)
                made[d] = copy_to(out.at[d], into.at[d], at_z(d))
            else:
                gtotal[:, lo:lo + n] = acc
        return made

    def grads_end(going, into, lo, n, scale):
        acc = gtotal[:, lo:lo + n]
        for d in near_z:
            going[d].wait_recv()
            acc = acc + decode_wide(into[d])
        gtotal[:, lo:lo + n] = acc * scale

    def ag_step(s):
        ag_right[s].wait_recv()
        ag_left[s].wait_recv()
        lo_y, hi_y = lax.rem(y - s + NY, NY), lax.rem(y + s, NY)
        size = rows if s < 3 else half
        piece = cot_at(lo_y, c, 0, size)
        ag_right[s + 1] = copy_to(piece, piece, at_y(1))
        piece = cot_at(hi_y, c, rows - size, size)
        ag_left[s + 1] = copy_to(piece, piece, at_y(-1))
        for yy in (lo_y, hi_y):
            piece = cot_at(yy, c, 0, rows)
            ag_mate.append(copy_to(piece, piece, mate))

    rs = {}

    def rs_rows(h):
        return pl.ds(0 if h == "A" else half, half)

    def rs_send(way, h, d):
        slot = len([k for k in rs if k[0] == way])
        target = rs_right if way > 0 else rs_left
        place = slot + (7 if way < 0 else 0)
        code, inverse = encode(base[(way * d) % NY, rs_rows(h), :])
        rs_out[place, :half, :] = code
        rs_out[place, half:, :] = jnp.broadcast_to(inverse, (16, 128)).astype(BF16)
        made = copy_to(rs_out.at[place], target.at[slot], at_y(way))
        rs[way, h, d] = (made, slot)

    def rs_take(way, h, d):
        made, slot = rs[way, h, d]
        made.wait_recv()
        source = rs_right if way > 0 else rs_left
        inverse = source[slot, half:half + 1, :].astype(F32)
        base[(way * (d - 1)) % NY, rs_rows(h), :] += decode(source[slot, :half, :], inverse)

    def rs_hop(d, first):
        right, left = ("A", "B") if first else ("B", "A")
        rs_take(1, right, d + 1)
        rs_send(1, right, d)
        rs_take(-1, left, d + 1)
        rs_send(-1, left, d)

    def through(yy):
        tgrad[...] += dot_nt(cotf[yy], w[:, pl.ds(pl.multiple_of(yy * 256, 256), 256)])

    def through_steps(*pieces):
        for i, s in pieces:
            ag_mate[i].wait_recv()
            through(lax.rem(y - s + NY, NY))

    maps_on("b", 1, 7)
    own_pair(pairs[0])
    maps_on("b", 2, 6)
    maps_on("a", 1, 7)
    tok_mate.wait_recv()
    mate_pair(pairs[0])
    rs_send(1, "A", 4)
    rs_send(-1, "B", 4)
    maps_on("b", 3, 5)
    maps_on("a", 2, 6)
    ag_step(1)
    maps_on("b", 4)
    rs_send(1, "B", 3)
    own_pair(pairs[1])
    mate_pair(pairs[1])
    rs_send(-1, "A", 3)
    maps_on("a", 3, 5)
    maps_on("a", 4)
    chosen_b = rank_start(0, "b", maps_b, cot)
    rs_hop(3, True)
    own_pair(pairs[2])
    ag_step(2)
    mate_pair(pairs[2])
    own_pair(pairs[3])
    chosen_a = rank_start(1, "a", maps_a, tok)
    rank_middle(0)
    rs_hop(2, False)
    mate_pair(pairs[3])
    for made in sel_x:
        made.wait_recv()
    cnt[0] = jnp.sum(jnp.sum(sel[...], axis=0), axis=0, keepdims=True)
    counted = [copy_to(cnt.at[0], cnt.at[k], at_z(k)) for k in range(1, NZ)]
    rs_hop(2, True)
    ag_step(3)
    rank_middle(1)
    rback = rank_end(0)
    going_a = grads_start(rback, tok, gxa, owna)
    rs_hop(1, False)
    rs_hop(1, True)
    ag_right[4].wait_recv()
    ag_left[4].wait_recv()
    far = cot_at(lax.rem(y + 4, NY), c, 0, rows)
    ag_mate.append(copy_to(far, far, mate))
    weights = owner_weights()
    ag_mate[0].wait_recv()
    tgrad[...] = dot_nt(cotf[y], w[:, pl.ds(pl.multiple_of(y * 256, 256), 256)])
    rin = rank_end(1)
    going_b = grads_start(rin, cot, gxb, ownb)
    going_a = grads_middle(weights, going_a, gxa, owna, za_out, za_in, 0)
    going_b = grads_middle(weights, going_b, gxb, ownb, zb_out, zb_in, feat)
    through_steps((1, 1), (2, -1))
    for b in range(nb):
        here = blocks_of(b)
        tgrad[here, :] += 2.0 * dot_tn(rback[b], jnp.concatenate([chosen_a[b]] * 2, axis=0))
        base[0, here, :] += 2.0 * dot_tn(rin[b], jnp.concatenate([chosen_b[b]] * 2, axis=0))
    rs_take(1, "B", 1)
    rs_take(-1, "A", 1)
    rs_take(1, "A", 1)
    rs_take(-1, "B", 1)
    out_pj = pltpu.make_async_copy(base.at[0], proj, lsem.at[1])
    out_pj.start()
    through_steps((3, 2), (4, -2), (5, 3), (6, -3), (7, 4))
    out_tg = pltpu.make_async_copy(tgrad, tgrad_out, lsem.at[0])
    out_tg.start()

    for made in counted:
        made.wait_recv()
    all_counts = jnp.sum(cnt[...], axis=0)
    mine = jnp.sum(jnp.where(lane == r, all_counts, 0.0), axis=1, keepdims=True)
    scale = 2.0 / jnp.maximum(mine * float(BLOCK), 1.0)
    grads_end(going_a, za_in, 0, feat, scale)
    grads_end(going_b, zb_in, feat, grouped - feat, scale)
    out_gi = pltpu.make_async_copy(gtotal.at[:, pl.ds(0, feat)], gin.at[0], lsem.at[2])
    out_go = pltpu.make_async_copy(gtotal.at[:, pl.ds(feat, grouped - feat)], gout.at[0], lsem.at[3])
    out_gi.start()
    out_go.start()
    for made in (out_tg, out_pj, out_gi, out_go):
        made.wait()
    for made in sent:
        made.wait_send()


def finish(*refs):
    n = 4
    sources, targets, held, came, gone = refs[:n], refs[n:2 * n], refs[2 * n:3 * n], refs[3 * n], refs[3 * n + 1]
    reads = [pltpu.make_async_copy(sources[i], held[i], came.at[i]) for i in range(n)]
    writes = [pltpu.make_async_copy(held[i], targets[i], gone.at[i]) for i in range(n)]
    for made in reads:
        made.start()
    for i in range(n):
        reads[i].wait()
        writes[i].start()
    for made in writes:
        made.wait()


COPIES = 224


def shards(tok, w, cot, ain, aout, tenant, storage):
    rows, feat = tok.shape
    cols = cot.shape[1]
    rank = ain.shape[1]
    nb = tenant.shape[0]
    grouped = feat + cols
    smem = pl.BlockSpec(memory_space=pltpu.SMEM)
    anywhere = pl.BlockSpec(memory_space=pl.ANY)
    shapes = ((rows, cols), (rows, feat), ain.shape, aout.shape)
    results = pl.pallas_call(
        kernel,
        out_shape=tuple(jax.ShapeDtypeStruct(shape, F32) for shape in shapes),
        in_specs=[smem, smem] + [anywhere] * 5,
        out_specs=[anywhere] * 4,
        scratch_shapes=[
            pltpu.VMEM((rows, feat), BF16),
            pltpu.VMEM(w.shape, BF16),
            pltpu.VMEM((rows, cols), BF16),
            pltpu.VMEM((rows, feat), F32),
            pltpu.VMEM((rank, grouped), F32),
            pltpu.VMEM((NX * NZ, rank, feat), BF16),
            pltpu.VMEM((NX * NZ, rank, cols), BF16),
            pltpu.VMEM((NX, nb, 128), F32),
            pltpu.VMEM((NZ, 1, 128), F32),
            pltpu.VMEM((NY, rows, NC * cols), BF16),
            pltpu.VMEM((rows, feat), BF16),
            pltpu.VMEM((NY, feat, cols), BF16),
            pltpu.VMEM((NY, rows, cols), F32),
            pltpu.VMEM((14, rows // 2 + 16, cols), BF16),
            pltpu.VMEM((7, rows // 2 + 16, cols), BF16),
            pltpu.VMEM((7, rows // 2 + 16, cols), BF16),
            pltpu.VMEM((2, NT, 4, 128), F32),
            pltpu.VMEM((2, NT, 4, 128), F32),
            pltpu.VMEM((2, NT, 4, 128), F32),
            pltpu.VMEM((NX, nb, rank, feat + 128), BF16),
            pltpu.VMEM((NX, nb, rank, cols + 128), BF16),
            pltpu.VMEM((NX * nb, rank, feat), F32),
            pltpu.VMEM((NX * nb, rank, cols), F32),
            pltpu.VMEM((NZ, rank, feat + 128), BF16),
            pltpu.VMEM((NZ, rank, cols + 128), BF16),
            pltpu.VMEM((NZ, rank, feat + 128), BF16),
            pltpu.VMEM((NZ, rank, cols + 128), BF16),
            pltpu.SemaphoreType.DMA((COPIES,)),
            pltpu.SemaphoreType.DMA((COPIES,)),
            pltpu.SemaphoreType.DMA((6,)),
        ],
        compiler_params=pltpu.CompilerParams(
            collective_id=0, has_side_effects=True, vmem_limit_bytes=VMEM_GRANT
        ),
    )(tenant, storage, tok, w, cot, ain, aout)
    return pl.pallas_call(
        finish,
        out_shape=tuple(jax.ShapeDtypeStruct(shape, F32) for shape in shapes),
        in_specs=[anywhere] * 4,
        out_specs=[anywhere] * 4,
        scratch_shapes=[pltpu.VMEM(shape, F32) for shape in shapes]
        + [pltpu.SemaphoreType.DMA((4,)), pltpu.SemaphoreType.DMA((4,))],
        compiler_params=pltpu.CompilerParams(vmem_limit_bytes=VMEM_GRANT),
    )(*results)


VMEM_GRANT = 63 * 1024 * 1024


def solution(mesh):
    placed = (
        P("rep", "tp"),
        P("tp", None),
        P("rep", "tp"),
        P("rep", None, "tp"),
        P("rep", None, "tp"),
        P("rep"),
        P(),
    )
    return jax.shard_map(
        shards,
        mesh=mesh,
        in_specs=placed,
        out_specs=(P("rep", "tp"), P("rep", "tp"), P("rep", None, "tp"), P("rep", None, "tp")),
        check_vma=False,
    )
```
